256 devices in a mesh: dp: 32 (over y, z), segment: 2 (over x_lo), chan: 4 (over x_hi, core).
Axes of the slice: x: 4 (x_hi: 2, x_lo: 2; x = x_hi * 2 + x_lo), y: 4, z: 8, core: 2. Of those that a mesh axis runs over, the one named last changes fastest.
Arguments:
- base: bfloat16 [64, 512, 256], P('dp', 'chan'), may hold values from -6 to 6
- style: float32 [2, 64, 512], P('segment', 'dp'), may hold values from -3 to 3
- noise: float32 [2, 64, 256], P('segment', 'dp'), may hold values from -6 to 6
- conv_weight: bfloat16 [2, 4608, 512], P('segment', None, 'chan'), may hold values from -0.09375 to 0.09375
- conv_bias: float32 [2, 512], P('segment', 'chan'), may hold values from -3 to 3
- noise_gain: float32 [2, 512], P('segment', 'chan'), may hold values from 0.1 to 1
- rgb_weight: bfloat16 [2, 3, 512], P('segment', None, 'chan'), may hold values from -0.25 to 0.25
- disc_weight: float32 [3, 256], replicated, may hold values from -3.5 to 3.5
- disc_bias: float32 [256], replicated, may hold values from -3 to 3
- disc_out: float32 [256], replicated, may hold values from -3 to 3
Outputs:
- conv_grad: float32 [2, 4608, 512], P('segment', 'dp', 'chan')
- logits: float32 [64], P('dp')
- section_input_grads: bfloat16 [2, 64, 512, 256], P('segment', 'dp', 'chan')
The draws below stay inside these ranges and needn't reach their ends.
All inputs are finite; a program needn't handle non-finite values.
Results may differ from the reference program's by a relative error of at most 0.015.
Values may be sent and summed in bfloat16 or wider, within the bound.
No kernel may reach another device: no remote copies, remote signals or barrier semaphores. Data moves between devices by JAX's collectives and lax.ppermute only.
A program may use at most 64 MiB of HBM per device.

```python
import math
import jax
import jax.numpy as jnp
from jax import lax

C = 512
CD = 256
RES = 16
PIX = 256
BATCH = 64


def draw_style(key, part):
    sign_key, size_key = jax.random.split(jax.random.fold_in(key, 11))
    sign_values = (2 * jax.random.randint(sign_key, (2, BATCH, C), 0, 2) - 1).astype(jnp.float32)
    exponent = jax.random.uniform(size_key, (2, BATCH, C), jnp.float32, math.log(0.3), math.log(3.0))
    magnitude = jnp.clip(jnp.exp(exponent), 0.3, 3.0)
    return sign_values * magnitude


def draw_conv_bias(key, part):
    first_key, second_key = jax.random.split(jax.random.fold_in(key, 23))
    first_row = jax.random.uniform(first_key, (C,), jnp.float32, -1.55, -1.25)
    second_row = jnp.clip(0.5 * jax.random.normal(second_key, (C,), jnp.float32), -3.0, 3.0)
    return jnp.stack([first_row, second_row])


def block_scale(key, dims, pieces, least, top_value):
    factor_of = 1.0
    for dim, parts in pieces:
        draws = jax.random.uniform(jax.random.fold_in(jax.random.fold_in(key, 6), dim), (parts,), jnp.float32, least / len(pieces), top_value / len(pieces))
        factor_of = factor_of * jnp.repeat(jnp.exp(draws), dims[dim] // parts).reshape((-1,) + (1,) * (len(dims) - 1 - dim))
    return factor_of


def scatter_about(stream_key, extent, scale, reach, cuts=(), kind=jnp.bfloat16):
    result = jax.random.normal(stream_key, extent, jnp.float32) * scale
    if len(cuts) > 0:
        result = block_scale(stream_key, extent, cuts, -0.22, 0.18) * result
    return jnp.clip(result, min=-reach, max=reach).astype(kind)


def setup_inputs(seed: int = 0) -> dict:
    streams_of = jax.random.split(jax.random.key(seed), 11)
    return {
        "base": scatter_about(streams_of[0], (BATCH, C, PIX), 1.0, 6.0, ((0, 32), (1, 4))),
        "style": draw_style(jax.random.fold_in(streams_of[10], 71), 0),
        "noise": scatter_about(streams_of[2], (2, BATCH, PIX), 1.0, 6.0, ((0, 2), (1, 32)), jnp.float32),
        "conv_weight": scatter_about(streams_of[3], (2, 9 * C, C), (9 * C) ** -0.5, 0.09375, ((0, 2), (2, 4))),
        "conv_bias": draw_conv_bias(jax.random.fold_in(streams_of[10], 71), 0),
        "noise_gain": jnp.clip(jnp.exp(math.log(1.0) - 2.3025851 * jax.random.uniform(streams_of[5], (2, C), jnp.float32) ** block_scale(streams_of[5], (2, C), ((0, 2), (1, 4)), -0.2, 0.2)), 0.1, 1.0),
        "rgb_weight": scatter_about(streams_of[6], (2, 3, C), C ** -0.5, 0.25, ((0, 2), (2, 4))),
        "disc_weight": scatter_about(streams_of[7], (3, CD), 3 ** -0.5, 3.5, (), jnp.float32),
        "disc_bias": scatter_about(streams_of[8], (CD,), 0.5, 3.0, (), jnp.float32),
        "disc_out": scatter_about(streams_of[9], (CD,), 0.5, 3.0, (), jnp.float32),
    }


epsilon = 1e-06
root_two = 1.4142135623730951
highest = lax.Precision.HIGHEST
kernel_offsets = [(ky - 1, kx - 1) for ky in range(3) for kx in range(3)]

def leaky_relu(values):
    return 0.2 * values + 0.8 * jax.nn.softplus(values)

def leaky_slope(values):
    return 0.2 + 0.8 * jax.nn.sigmoid(values)

def shift_grid(values, offset_y, offset_x):
    leading = values.shape[:-1]
    planes = values.reshape(leading + (RES, RES))
    padded = jnp.pad(planes, [(0, 0)] * len(leading) + [(1, 1), (1, 1)])
    moved = padded[..., 1 + offset_y:1 + offset_y + RES, 1 + offset_x:1 + offset_x + RES]
    return moved.reshape(leading + (RES * RES,))

def unfold(modulated):
    return jnp.concatenate([shift_grid(modulated, oy, ox) for oy, ox in kernel_offsets], axis=0)

def fold_back(columns, channels):
    total = jnp.zeros((channels, RES * RES), columns.dtype)
    for kernel_pos, (oy, ox) in enumerate(kernel_offsets):
        total = total + shift_grid(columns[kernel_pos * channels:(kernel_pos + 1) * channels], -oy, -ox)
    return total

def section_forward(inputs, style_row, noise_row, weight, bias_row, gain_row):
    w_float = weight.astype(jnp.float32)
    squares = lax.optimization_barrier(jnp.sum((w_float * w_float).reshape(9, C, C), axis=0))
    demod = lax.rsqrt(jnp.dot(style_row * style_row, squares, precision=highest, preferred_element_type=jnp.float32) + epsilon)
    modulated = (inputs.astype(jnp.float32) * style_row[:, None]).astype(jnp.bfloat16)
    columns = unfold(modulated)
    conv_out = lax.dot_general(weight, columns, (((0,), (0,)), ((), ())), preferred_element_type=jnp.float32)
    pre_act = demod[:, None] * conv_out + gain_row[:, None] * noise_row[None, :] + bias_row[:, None]
    out_act = (root_two * leaky_relu(pre_act)).astype(jnp.bfloat16)
    return (out_act, pre_act, conv_out, demod, columns)

def section_backward(grad_out, pre_act, conv_out, demod, weight, style_row, columns):
    d_act = grad_out * root_two * leaky_slope(pre_act)
    d_conv = (d_act * demod[:, None]).astype(jnp.bfloat16)
    d_demod = lax.optimization_barrier(jnp.sum(d_act * conv_out, axis=1))
    coef = -d_demod * demod * demod * demod
    d_columns = lax.dot_general(weight, d_conv, (((1,), (0,)), ((), ())), preferred_element_type=jnp.float32)
    d_input = fold_back(d_columns, C)
    returned = (d_input * style_row[:, None]).astype(jnp.bfloat16)
    w_float = weight.astype(jnp.float32)
    outer = (style_row * style_row)[:, None] * coef[None, :]
    grad = lax.dot_general(columns, d_conv, (((1,), (1,)), ((), ())), preferred_element_type=jnp.float32)
    grad = grad + (w_float.reshape(9, C, C) * outer[None]).reshape(9 * C, C)
    return (returned, grad)

def reference(base, style, noise, conv_weight, conv_bias, noise_gain, rgb_weight, disc_weight, disc_bias, disc_out):
    styles = jnp.swapaxes(style, 0, 1)
    noises = jnp.swapaxes(noise, 0, 1)

    def one_sample(carry, items):
        sample_base, sample_style, sample_noise = items
        first = section_forward(sample_base, sample_style[0], sample_noise[0], conv_weight[0], conv_bias[0], noise_gain[0])
        second = section_forward(first[0], sample_style[1], sample_noise[1], conv_weight[1], conv_bias[1], noise_gain[1])
        image = jnp.dot(rgb_weight[0], first[0], preferred_element_type=jnp.float32)
        image = image + jnp.dot(rgb_weight[1], second[0], preferred_element_type=jnp.float32)
        pre_disc = jnp.einsum('cj,cp->jp', disc_weight, image, precision=highest) + disc_bias[:, None]
        hidden = leaky_relu(pre_disc)
        logit = jnp.dot(disc_out, lax.optimization_barrier(jnp.mean(hidden, axis=1)), precision=highest)
        grad_logit = jax.nn.sigmoid(logit) - 1.0
        d_pre = grad_logit * disc_out[:, None] / (RES * RES) * leaky_slope(pre_disc)
        d_image = jnp.einsum('cj,jp->cp', disc_weight, d_pre, precision=highest)
        head_second = jnp.einsum('co,cp->op', rgb_weight[1].astype(jnp.float32), d_image, precision=highest)
        head_first = jnp.einsum('co,cp->op', rgb_weight[0].astype(jnp.float32), d_image, precision=highest)
        returned, grad_second = section_backward(head_second, second[1], second[2], second[3], conv_weight[1], sample_style[1], second[4])
        grad_in = head_first + returned.astype(jnp.float32)
        first_returned, grad_first = section_backward(grad_in, first[1], first[2], first[3], conv_weight[0], sample_style[0], first[4])
        return ((carry[0] + grad_first, carry[1] + grad_second), (logit, jnp.stack([first_returned, returned])))
    zeros = jnp.zeros((9 * C, C), jnp.float32)
    totals, outputs = lax.scan(one_sample, (zeros, zeros), (base, styles, noises))
    logits, input_grads = outputs
    return (jnp.stack([totals[0], totals[1]]), logits, jnp.swapaxes(input_grads, 0, 1))
```

```python
import functools

import jax
import jax.numpy as jnp
from jax import lax
from jax.experimental import pallas as pl
from jax.experimental.pallas import tpu as pltpu
from jax.sharding import PartitionSpec as P

RES = 16
PIX = RES * RES
TAPS = 9
EXTRA = 16
epsilon = 1e-06
root_two = 1.4142135623730951
f32 = jnp.float32
bf16 = jnp.bfloat16


NT = (((1,), (1,)), ((), ()))


def act_parts(t):
    e = jnp.exp(-jnp.abs(t))
    r = 1.0 / (1.0 + e)
    soft = jnp.maximum(t, 0.0) + jnp.log(1.0 + e)
    sig = jnp.where(t >= 0.0, r, e * r)
    return soft, sig


def row_shift(v, a):
    if a == 0:
        return v
    zeros = jnp.zeros((RES, v.shape[1]), v.dtype)
    parts = []
    for b in range(v.shape[0] // PIX):
        base = b * PIX
        if a > 0:
            parts += [v[base + RES : base + PIX], zeros]
        else:
            parts += [zeros, v[base : base + PIX - RES]]
    return jnp.concatenate(parts, axis=0)


def col_shift(v, b):
    if b == 0:
        return v
    x = lax.broadcasted_iota(jnp.int32, v.shape, 0) & (RES - 1)
    if b > 0:
        return jnp.where(x < RES - 1, pltpu.roll(v, v.shape[0] - 1, 0), 0.0)
    return jnp.where(x > 0, pltpu.roll(v, 1, 0), 0.0)


def split_two(v):
    hi = v.astype(bf16)
    lo = (v - hi.astype(f32)).astype(bf16)
    return hi, lo


def pad_rows(v, rows):
    return jnp.concatenate([v, jnp.zeros((rows - v.shape[0], v.shape[1]), v.dtype)], axis=0)


def base_kernel(base_ref, out_ref):
    for b in range(base_ref.shape[0]):
        out_ref[b * PIX : (b + 1) * PIX, :] = base_ref[b].T


def prep_kernel(
    idx, w_ref, sty_ref, noise_ref, gain_ref, bias_ref, dw_ref, db_ref, do_ref,
    wslot_ref, stys_ref, demod_ref, nb_ref, disc_ref,
):
    chan = idx[1]
    own = w_ref.shape[1]
    full = w_ref.shape[0] // TAPS
    count = sty_ref.shape[0]
    chans = full // own
    for d in range(chans):
        part = chan ^ d
        for k in range(TAPS):
            start = pl.multiple_of(k * full + part * own, own)
            wslot_ref[d * own : (d + 1) * own, k * own : (k + 1) * own] = w_ref[pl.ds(start, own), :]
        stys_ref[:, d * own : (d + 1) * own] = sty_ref[:, pl.ds(pl.multiple_of(part * own, own), own)]
    squares = jnp.zeros((full, own), f32)
    for k in range(TAPS):
        w = w_ref[k * full : (k + 1) * full, :].astype(f32)
        squares = squares + w * w
    sty = sty_ref[...]
    cols = pad_rows(sty * sty, own).T
    for b in range(count):
        total = jnp.sum(cols[:, b : b + 1] * squares, axis=0, keepdims=True)
        demod_ref[b : b + 1, :] = lax.rsqrt(total + epsilon)
        noise = jnp.broadcast_to(noise_ref[b : b + 1, :], (own, PIX)).T
        nb_ref[b * PIX : (b + 1) * PIX, :] = gain_ref[...] * noise + bias_ref[...]
    rows = [dw_ref[0:1, :], dw_ref[1:2, :], dw_ref[2:3, :], db_ref[...], do_ref[...]]
    for n, row in enumerate(rows):
        disc_ref[n] = jnp.broadcast_to(row, (own, row.shape[1])).T


def conv_kernel(with_image, *refs):
    x_refs = refs[:4]
    stys_ref, wslot_ref, demod_ref, nb_ref, rgb_ref = refs[4:9]
    pay_ref, slope_ref, z_ref, xm_ref = refs[9:13]
    count = stys_ref.shape[0]
    own = demod_ref.shape[1]
    pixels = count * PIX
    for d in range(4):
        for b in range(count):
            sty = stys_ref[b : b + 1, d * own : (d + 1) * own]
            x = x_refs[d][b * PIX : (b + 1) * PIX, :].astype(f32)
            xm_ref[b * PIX : (b + 1) * PIX, d * own : (d + 1) * own] = (x * sty).astype(bf16)
    products = jnp.dot(xm_ref[...], wslot_ref[...], preferred_element_type=f32)
    z = None
    for kx in range(3):
        total = None
        for ky in range(3):
            k = 3 * ky + kx
            moved = row_shift(products[:, k * own : (k + 1) * own], ky - 1)
            total = moved if total is None else total + moved
        total = col_shift(total, kx - 1)
        z = total if z is None else z + total
    z_ref[...] = z
    demod = jnp.concatenate(
        [jnp.broadcast_to(demod_ref[b : b + 1, :], (PIX, own)) for b in range(count)], axis=0
    )
    pre = demod * z + nb_ref[...]
    soft, sig = act_parts(pre)
    y = (root_two * (0.2 * pre + 0.8 * soft)).astype(bf16)
    slope_ref[...] = root_two * (0.2 + 0.8 * sig)
    rgb = pad_rows(rgb_ref[...], EXTRA)
    pay_ref[:pixels, :] = y
    pay_ref[pixels:, :] = rgb
    if with_image:
        own_ref, first_ref = refs[13:15]
        own_ref[...] = lax.dot_general(rgb, y, NT, preferred_element_type=f32)[:8]
        parts = [
            lax.dot_general(
                x_refs[d][pixels:, :], x_refs[d][:pixels, :], NT, preferred_element_type=f32
            )[:8]
            for d in range(4)
        ]
        first_ref[...] = (parts[0] + parts[1]) + (parts[2] + parts[3])


def head_grad(dimage, rgb_ref):
    own = rgb_ref.shape[1]
    hi = dimage.astype(bf16).astype(f32)
    lo = dimage - hi
    left = pad_rows(jnp.concatenate([hi, lo], axis=0), own).T.astype(bf16)
    rgb = rgb_ref[...].astype(f32)
    right = jnp.concatenate([pad_rows(rgb, 8), pad_rows(rgb, 8)], axis=0)
    return jnp.dot(left, pad_rows(right, own).astype(bf16), preferred_element_type=f32)


def store_gz(da, z, demod_ref, pay_ref):
    count, own = demod_ref.shape
    rows = []
    for b in range(count):
        demod = demod_ref[b : b + 1, :]
        part = da[b * PIX : (b + 1) * PIX]
        pay_ref[b * PIX : (b + 1) * PIX, :] = (part * demod).astype(bf16)
        d_demod = jnp.sum(part * z[b * PIX : (b + 1) * PIX], axis=0, keepdims=True)
        rows.append(-d_demod * demod * demod * demod)
    coef = jnp.concatenate(rows + [jnp.zeros((8 - count, own), f32)], axis=0)
    hi = coef.astype(bf16).astype(f32)
    pay_ref[count * PIX :, :] = jnp.concatenate([hi, coef - hi], axis=0).astype(bf16)


def store_dx(gz, wslot_ref, stys_ref, out_refs):
    count = stys_ref.shape[0]
    own = gz.shape[1]
    gz = gz.astype(f32)
    by_col = [col_shift(gz, 1 - kx).astype(bf16) for kx in range(3)]
    cols = jnp.concatenate(
        [row_shift(by_col[k % 3], 1 - k // 3) for k in range(TAPS)], axis=1
    )
    share = lax.dot_general(cols, wslot_ref[...], NT, preferred_element_type=f32)
    for d in range(4):
        for b in range(count):
            sty = stys_ref[b : b + 1, d * own : (d + 1) * own]
            out_refs[d][b * PIX : (b + 1) * PIX, :] = (
                share[b * PIX : (b + 1) * PIX, d * own : (d + 1) * own] * sty
            ).astype(bf16)


def disc_kernel(
    own_ref, r1_ref, r2_ref, r3_ref, first_ref, disc_ref, rgb_ref, slope_ref, z_ref, demod_ref,
    wslot_ref, stys_ref, dimg_ref, pay_ref, *out_refs,
):
    image = ((own_ref[...] + r1_ref[...]) + (r2_ref[...] + r3_ref[...])) + first_ref[...]
    lanes = 128
    per = PIX // lanes
    count = stys_ref.shape[0]
    out_rows = []
    for b in range(count):
        logit = jnp.zeros((1, 1), f32)
        chunks = []
        for n in range(per):
            at = b * PIX + n * lanes
            q = disc_ref[3]
            for ch in range(3):
                q = q + disc_ref[ch] * image[ch : ch + 1, at : at + lanes]
            soft, sig = act_parts(q)
            hidden = 0.2 * q + 0.8 * soft
            logit = logit + jnp.sum(disc_ref[4] * hidden, keepdims=True)
            dq = (disc_ref[4] / PIX) * (0.2 + 0.8 * sig)
            chunks.append(
                [jnp.sum(disc_ref[ch] * dq, axis=0, keepdims=True) for ch in range(3)]
            )
        logit = logit / PIX
        e = jnp.exp(-jnp.abs(logit))
        g = -jnp.where(logit >= 0.0, e, 1.0) / (1.0 + e)
        wide = jnp.broadcast_to(logit, (1, PIX))
        rows = [jnp.concatenate([c[ch] for c in chunks], axis=1) * g for ch in range(3)]
        out_rows.append(jnp.concatenate(rows + [jnp.zeros((5, PIX), f32)], axis=0))
        row_id = lax.broadcasted_iota(jnp.int32, (8, PIX), 0)
        dimg_ref[:, b * PIX : (b + 1) * PIX] = jnp.where(
            row_id == 3, jnp.broadcast_to(logit, (8, PIX)), out_rows[-1]
        )
    dimage = jnp.concatenate(out_rows, axis=1)
    da = head_grad(dimage, rgb_ref) * slope_ref[...]
    store_gz(da, z_ref[...], demod_ref, pay_ref)
    store_dx(pay_ref[: count * PIX, :], wslot_ref, stys_ref, out_refs)


def first_grad_kernel(
    idx, s0_ref, s1_ref, s2_ref, s3_ref, dimg_ref, rgb_ref, slope_ref, z_ref, demod_ref, other_ref,
    pay_ref, dx_ref,
):
    @pl.when(idx[0] == 0)
    def _():
        total = (s0_ref[...].astype(f32) + s1_ref[...].astype(f32)) + (
            s2_ref[...].astype(f32) + s3_ref[...].astype(f32)
        )
        dx = total.astype(bf16)
        dx_ref[...] = dx
        row_id = lax.broadcasted_iota(jnp.int32, dimg_ref.shape, 0)
        dimage = jnp.where(row_id < 3, dimg_ref[...], 0.0)
        da = (head_grad(dimage, rgb_ref) + dx.astype(f32)) * slope_ref[...]
        store_gz(da, z_ref[...], demod_ref, pay_ref)

    @pl.when(idx[0] != 0)
    def _():
        pay_ref[...] = other_ref[...]
        dx_ref[...] = jnp.zeros_like(dx_ref)


def share_kernel(pay_ref, wslot_ref, stys_ref, *out_refs):
    pixels = stys_ref.shape[0] * PIX
    store_dx(pay_ref[:pixels, :], wslot_ref, stys_ref, out_refs)


def turn_kernel(idx, xa_ref, xb_ref, sty_ref, out_ref):
    chan = idx[1]
    full = xa_ref.shape[1]
    count = sty_ref.shape[0]
    own = full // 4

    def turn(ref):
        for d in range(4):
            start = pl.multiple_of((chan ^ d) * own, own)
            out_ref[pl.ds(start, own), :] = ref[:, d * own : (d + 1) * own].T

    @pl.when(idx[0] == 0)
    def _():
        turn(xa_ref)

    @pl.when(idx[0] != 0)
    def _():
        turn(xb_ref)

    sty = sty_ref[...]
    hi = sty.astype(bf16).astype(f32)
    mid = (sty - hi).astype(bf16).astype(f32)
    lo = sty - hi - mid
    rows = [hi, mid, lo]
    out_ref[full:, :] = jnp.concatenate(
        rows + [jnp.zeros((EXTRA - 3 * count, full), f32)], axis=0
    ).astype(bf16)


def weight_kernel(idx, *refs):
    pays, xms, w_ref = refs[:4], refs[4:8], refs[8]
    outs = refs[9:17]
    g_ref, sum_ref = refs[17:19]
    y, z = idx[2], idx[3]
    full = xms[0].shape[0] - EXTRA
    own = pays[0].shape[1]
    pixels = pays[0].shape[0] - EXTRA
    count = pixels // PIX
    stride = PIX + 2 * RES
    zeros = jnp.zeros((RES, own), bf16)
    for n in range(4):
        gz = pays[n][:pixels, :].astype(f32)
        for kx in range(3):
            moved = col_shift(gz, 1 - kx).astype(bf16)
            for b in range(count):
                at = (n * count + b) * stride
                g_ref[kx, at : at + RES, :] = zeros
                g_ref[kx, at + RES : at + RES + PIX, :] = moved[b * PIX : (b + 1) * PIX]
                g_ref[kx, at + RES + PIX : at + stride, :] = zeros
    total = None
    for n in range(4):
        taps = []
        for j in range(3):
            k = 2 * y + j
            ky = k // 3
            kx = k - 3 * ky
            rows = []
            for b in range(count):
                start = (n * count + b) * stride + (2 - ky) * RES
                rows.append(g_ref[kx, pl.ds(pl.multiple_of(start, RES), PIX), :])
            taps.append(jnp.concatenate(rows, axis=0))
        part = jnp.dot(
            xms[n][:full, :], jnp.concatenate(taps, axis=1), preferred_element_type=f32
        )
        total = part if total is None else total + part
    sty_rows, coef_rows = [], []
    for n in range(4):
        tail = xms[n][full:, :].astype(f32)
        sty = tail[:count] + tail[count : 2 * count] + tail[2 * count : 3 * count]
        sty_rows.append(sty * sty)
        tail = pays[n][pixels:, :].astype(f32)
        coef_rows.append(tail[:count] + tail[8 : 8 + count])
    left = pad_rows(jnp.concatenate(sty_rows, axis=0), own).T
    right = pad_rows(jnp.concatenate(coef_rows, axis=0), own)
    demod_term = jnp.dot(left, right, precision=lax.Precision.HIGHEST, preferred_element_type=f32)
    for j in range(3):
        start = pl.multiple_of((2 * y + j) * full, full)
        w = w_ref[pl.ds(start, full), :].astype(f32)
        sum_ref[j * full : (j + 1) * full, :] = (
            total[:, j * own : (j + 1) * own] + w * demod_term
        ).astype(bf16)
    rows = outs[0].shape[0]
    for d in range(8):
        start = y * own + ((z + d) & 7) * rows
        outs[d][...] = sum_ref[pl.ds(pl.multiple_of(start, RES), rows), :]


def total_kernel(*refs):
    total = refs[0][...].astype(f32)
    for ref in refs[1:-1]:
        total = total + ref[...].astype(f32)
    refs[-1][...] = total


def input_grad_kernel(idx, s0_ref, s1_ref, s2_ref, s3_ref, back_ref, out_ref):
    def put(dx):
        for b in range(out_ref.shape[0]):
            out_ref[b] = dx[b * PIX : (b + 1) * PIX].T

    @pl.when(idx[0] == 0)
    def _():
        total = (s0_ref[...].astype(f32) + s1_ref[...].astype(f32)) + (
            s2_ref[...].astype(f32) + s3_ref[...].astype(f32)
        )
        put(total.astype(bf16))

    @pl.when(idx[0] != 0)
    def _():
        put(back_ref[...])


def call(kernel, outs, args, scratch=(), scalars=0, name=None):
    smem = pl.BlockSpec(memory_space=pltpu.SMEM)
    vmem = pl.BlockSpec(memory_space=pltpu.VMEM)
    out = pl.pallas_call(
        kernel,
        out_shape=[jax.ShapeDtypeStruct(s, t) for s, t in outs],
        in_specs=[smem] * scalars + [vmem] * (len(args) - scalars),
        out_specs=[vmem] * len(outs),
        scratch_shapes=list(scratch),
        name=name,
    )(*args)
    return out


def shards(
    base, style, noise, conv_weight, conv_bias, noise_gain, rgb_weight, disc_weight, disc_bias,
    disc_out,
):
    weight, styles, noises, rgb = conv_weight[0], style[0], noise[0], rgb_weight[0]
    own = weight.shape[1]
    full = weight.shape[0] // TAPS
    count = base.shape[0]
    pixels = count * PIX
    dp_index = lax.axis_index("dp")
    idx = jnp.stack(
        [lax.axis_index("segment"), lax.axis_index("chan"), dp_index // 8, dp_index % 8]
    ).astype(jnp.int32)

    def across(value, links):
        return lax.ppermute(value, ("segment", "chan"), links)

    def over_y(value, d):
        return lax.ppermute(
            value, "dp", [(y * 8 + z, (y + d) % 4 * 8 + z) for y in range(4) for z in range(8)]
        )

    def over_z(value, d):
        return lax.ppermute(
            value, "dp", [(y * 8 + z, y * 8 + (z + d) % 8) for y in range(4) for z in range(8)]
        )

    four = range(4)
    (x0,) = call(base_kernel, [((pixels, own), bf16)], [base], name="base")
    x3 = across(x0, [(4 + (c ^ 3), c) for c in four])
    x2 = across(x0, [(4 + (c ^ 2), c) for c in four])
    x1 = across(x0, [(c ^ 1, c) for c in four])
    wslot, stys, demod, nb, disc = call(
        prep_kernel,
        [
            ((full, TAPS * own), bf16),
            ((count, full), f32),
            ((count, own), f32),
            ((pixels, own), f32),
            ((5, disc_weight.shape[1], own), f32),
        ],
        [
            idx, weight, styles, noises, noise_gain, conv_bias, disc_weight, disc_bias[None],
            disc_out[None],
        ],
        scalars=1,
        name="prep",
    )
    conv_outs = [
        ((pixels + EXTRA, own), bf16),
        ((pixels, own), f32),
        ((pixels, own), f32),
        ((pixels, full), bf16),
    ]
    pay, slope_a, z_a, xm_a = call(
        functools.partial(conv_kernel, False),
        conv_outs,
        [x0, x1, x2, x3, stys, wslot, demod, nb, rgb],
        name="conv_first",
    )
    slots = [across(pay, [(c ^ d, 4 + c) for c in four]) for d in four]
    _, slope_b, z_b, xm_b, image_own, image_first = call(
        functools.partial(conv_kernel, True),
        conv_outs + [((8, pixels), f32), ((8, pixels), f32)],
        [*slots, stys, wslot, demod, nb, rgb],
        name="conv_second",
    )
    images = [across(image_own, [(4 + (c ^ d), 4 + c) for c in four]) for d in (1, 2, 3)]
    (xm,) = call(
        turn_kernel, [((full + EXTRA, pixels), bf16)], [idx, xm_a, xm_b, styles], scalars=1,
        name="turn",
    )
    xms = [xm] + [over_y(xm, d) for d in (1, 2, 3)]
    share = ((pixels, own), bf16)
    dimg, pay_b, *shares = call(
        disc_kernel,
        [((8, pixels), f32), ((pixels + EXTRA, own), bf16)] + [share] * 4,
        [image_own, *images, image_first, disc, rgb, slope_b, z_b, demod, wslot, stys],
        name="disc",
    )
    dimg_a = across(dimg, [(4 + c, c) for c in four])
    got = [across(shares[d], [(4 + c, c ^ d) for c in four]) for d in four]
    pay_g, dx_b = call(
        first_grad_kernel,
        [((pixels + EXTRA, own), bf16), share],
        [idx, *got, dimg_a, rgb, slope_a, z_a, demod, pay_b],
        scalars=1,
        name="first_grad",
    )
    pays = [pay_g] + [over_y(pay_g, d) for d in (1, 2, 3)]
    shares = call(share_kernel, [share] * 4, [pay_g, wslot, stys], name="share")
    mine = [shares[0]] + [
        across(shares[d], [(c, c ^ d) for c in four]) for d in (1, 2, 3)
    ]
    back = across(dx_b, [(c, 4 + c) for c in four])
    rows = weight.shape[0] // 32
    blocks = call(
        weight_kernel,
        [((rows, own), bf16)] * 8,
        [idx, *pays, *xms, weight],
        scratch=[
            pltpu.VMEM((3, 4 * count * (PIX + 2 * RES), own), bf16),
            pltpu.VMEM((3 * full, own), bf16),
        ],
        scalars=1,
        name="weight_grad",
    )
    parts = [blocks[0]] + [over_z(blocks[d], d) for d in range(1, 8)]
    (grad_rows,) = call(total_kernel, [((rows, own), f32)], parts, name="total")
    (dx,) = call(
        input_grad_kernel, [((count, own, PIX), bf16)], [idx, *mine, back], scalars=1,
        name="input_grad",
    )
    logits = jnp.where(lax.axis_index("segment") == 0, dimg_a[3, ::PIX], dimg[3, ::PIX])
    return (grad_rows[None], logits, dx[None])


def solution(mesh):
    placed = (
        P("dp", "chan", None),
        P("segment", "dp", None),
        P("segment", "dp", None),
        P("segment", None, "chan"),
        P("segment", "chan"),
        P("segment", "chan"),
        P("segment", None, "chan"),
        P(),
        P(),
        P(),
    )
    return jax.shard_map(
        shards,
        mesh=mesh,
        in_specs=placed,
        out_specs=(P("segment", "dp", "chan"), P("dp"), P("segment", "dp", "chan", None)),
        check_vma=False,
    )
```

```python
import functools

import jax
import jax.numpy as jnp
from jax import lax
from jax.experimental import pallas as pl
from jax.experimental.pallas import tpu as pltpu
from jax.sharding import PartitionSpec as P


RES = 16
PIX = RES * RES
TAPS = 9
EXTRA = 16
TAIL = 32
epsilon = 1e-06
root_two = 1.4142135623730951
f32 = jnp.float32
bf16 = jnp.bfloat16


NT = (((1,), (1,)), ((), ()))


def act_parts(t):
    e = jnp.exp(-jnp.abs(t))
    r = 1.0 / (1.0 + e)
    soft = jnp.maximum(t, 0.0) + jnp.log(1.0 + e)
    sig = jnp.where(t >= 0.0, r, e * r)
    return soft, sig


def row_shift(v, a):
    if a == 0:
        return v
    zeros = jnp.zeros((RES, v.shape[1]), v.dtype)
    parts = []
    for b in range(v.shape[0] // PIX):
        base = b * PIX
        if a > 0:
            parts += [v[base + RES : base + PIX], zeros]
        else:
            parts += [zeros, v[base : base + PIX - RES]]
    return jnp.concatenate(parts, axis=0)


def col_shift(v, b):
    if b == 0:
        return v
    x = lax.broadcasted_iota(jnp.int32, v.shape, 0) & (RES - 1)
    if b > 0:
        return jnp.where(x < RES - 1, pltpu.roll(v, v.shape[0] - 1, 0), 0.0)
    return jnp.where(x > 0, pltpu.roll(v, 1, 0), 0.0)


def pad_rows(v, rows):
    return jnp.concatenate([v, jnp.zeros((rows - v.shape[0], v.shape[1]), v.dtype)], axis=0)


def prep_kernel(idx, *refs):
    number = (len(refs) - 8) // 2
    sources, outs, copies = refs[:number], refs[number : number + 7], refs[number + 7 : -1]
    sem = refs[-1]
    moves = [
        pltpu.make_async_copy(src, dst, sem.at[n]) for n, (src, dst) in enumerate(zip(sources, copies))
    ]
    for move in moves:
        move.start()
    for move in moves:
        move.wait()
    w_ref, sty_ref, noise_ref, gain_ref, bias_ref, dw_ref, db_ref, do_ref, rgb_ref = copies
    wslot_ref, stys_ref, demod_ref, nb_ref, disc_ref, rgbp_ref, stycopy_ref = outs
    rgbp_ref[...] = pad_rows(rgb_ref[...], EXTRA)
    stycopy_ref[...] = sty_ref[...]
    chan = idx[1]
    own = w_ref.shape[1]
    full = w_ref.shape[0] // TAPS
    count = sty_ref.shape[0]
    chans = full // own
    for d in range(chans):
        part = chan ^ d
        for k in range(TAPS):
            start = pl.multiple_of(k * full + part * own, own)
            wslot_ref[d * own : (d + 1) * own, k * own : (k + 1) * own] = w_ref[pl.ds(start, own), :]
        stys_ref[:, d * own : (d + 1) * own] = sty_ref[:, pl.ds(pl.multiple_of(part * own, own), own)]
    squares = jnp.zeros((full, own), f32)
    for k in range(TAPS):
        w = w_ref[k * full : (k + 1) * full, :].astype(f32)
        squares = squares + w * w
    sty = sty_ref[...]
    cols = pad_rows(sty * sty, own).T
    for b in range(count):
        total = jnp.sum(cols[:, b : b + 1] * squares, axis=0, keepdims=True)
        demod_ref[b : b + 1, :] = lax.rsqrt(total + epsilon)
        noise = jnp.broadcast_to(noise_ref[b : b + 1, :], (own, PIX)).T
        nb_ref[b * PIX : (b + 1) * PIX, :] = gain_ref[...] * noise + bias_ref[...]
    rows = [dw_ref[0:1, :], dw_ref[1:2, :], dw_ref[2:3, :], db_ref[...], do_ref[...]]
    for n, row in enumerate(rows):
        disc_ref[n] = jnp.broadcast_to(row, (own, row.shape[1])).T


def conv_kernel(second, *refs):
    x_refs = refs[:4]
    stys_ref, wslot_ref, demod_ref, nb_ref, rgb_ref = refs[4:9]
    pay_ref, slope_ref, z_ref, xm_ref = refs[9:13]
    count = stys_ref.shape[0]
    own = demod_ref.shape[1]
    pixels = count * PIX
    for d in range(4):
        for b in range(count):
            sty = stys_ref[b : b + 1, d * own : (d + 1) * own]
            x = x_refs[d][b * PIX : (b + 1) * PIX, :] if second else x_refs[d][b].T
            x = x.astype(f32)
            xm_ref[b * PIX : (b + 1) * PIX, d * own : (d + 1) * own] = (x * sty).astype(bf16)
    products = jnp.dot(xm_ref[...], wslot_ref[...], preferred_element_type=f32)
    z = None
    for kx in range(3):
        total = None
        for ky in range(3):
            k = 3 * ky + kx
            moved = row_shift(products[:, k * own : (k + 1) * own], ky - 1)
            total = moved if total is None else total + moved
        total = col_shift(total, kx - 1)
        z = total if z is None else z + total
    z_ref[...] = z
    demod = jnp.concatenate(
        [jnp.broadcast_to(demod_ref[b : b + 1, :], (PIX, own)) for b in range(count)], axis=0
    )
    pre = demod * z + nb_ref[...]
    soft, sig = act_parts(pre)
    y = (root_two * (0.2 * pre + 0.8 * soft)).astype(bf16)
    slope_ref[...] = root_two * (0.2 + 0.8 * sig)
    rgb = rgb_ref[...]
    pay_ref[:pixels, :] = y
    pay_ref[pixels:, :] = rgb
    if second:
        refs[13][...] = lax.dot_general(rgb, y, NT, preferred_element_type=f32)[:8]


def first_image_kernel(*refs):
    out_ref = refs[-1]
    pixels = out_ref.shape[1]
    parts = [
        lax.dot_general(ref[pixels:, :], ref[:pixels, :], NT, preferred_element_type=f32)[:8]
        for ref in refs[:4]
    ]
    out_ref[...] = (parts[0] + parts[1]) + (parts[2] + parts[3])


def head_grad(dimage, rgb_ref):
    own = rgb_ref.shape[1]
    hi = dimage.astype(bf16).astype(f32)
    lo = dimage - hi
    left = pad_rows(jnp.concatenate([hi, lo], axis=0), own).T.astype(bf16)
    rgb = rgb_ref[...].astype(f32)[:8]
    right = jnp.concatenate([rgb, rgb], axis=0)
    return jnp.dot(left, pad_rows(right, own).astype(bf16), preferred_element_type=f32)


def store_gz(da, z, demod_ref, pay_ref):
    count, own = demod_ref.shape
    rows = []
    for b in range(count):
        demod = demod_ref[b : b + 1, :]
        part = da[b * PIX : (b + 1) * PIX]
        pay_ref[b * PIX : (b + 1) * PIX, :] = (part * demod).astype(bf16)
        d_demod = jnp.sum(part * z[b * PIX : (b + 1) * PIX], axis=0, keepdims=True)
        rows.append(-d_demod * demod * demod * demod)
    coef = jnp.concatenate(rows + [jnp.zeros((8 - count, own), f32)], axis=0)
    hi = coef.astype(bf16).astype(f32)
    pay_ref[count * PIX :, :] = jnp.concatenate([hi, coef - hi], axis=0).astype(bf16)


def store_dx(gz, wslot_ref, stys_ref, put):
    count = stys_ref.shape[0]
    own = gz.shape[1]
    gz = gz.astype(f32)
    by_col = [col_shift(gz, 1 - kx).astype(bf16) for kx in range(3)]
    cols = jnp.concatenate(
        [row_shift(by_col[k % 3], 1 - k // 3) for k in range(TAPS)], axis=1
    )
    share = lax.dot_general(cols, wslot_ref[...], NT, preferred_element_type=f32)
    for d in range(4):
        for b in range(count):
            sty = stys_ref[b : b + 1, d * own : (d + 1) * own]
            put(d, b, share[b * PIX : (b + 1) * PIX, d * own : (d + 1) * own] * sty)


def disc_kernel(
    own_ref, r1_ref, r2_ref, r3_ref, first_ref, disc_ref, rgb_ref, slope_ref, z_ref, demod_ref,
    wslot_ref, stys_ref, tail_ref, pay_ref, keep_ref, send_ref,
):
    image = ((own_ref[...] + r1_ref[...]) + (r2_ref[...] + r3_ref[...])) + first_ref[...]
    lanes = 128
    per = PIX // lanes
    count = stys_ref.shape[0]
    out_rows, logits = [], []
    for b in range(count):
        logit = jnp.zeros((1, 1), f32)
        chunks = []
        for n in range(per):
            at = b * PIX + n * lanes
            q = disc_ref[3]
            for ch in range(3):
                q = q + disc_ref[ch] * image[ch : ch + 1, at : at + lanes]
            soft, sig = act_parts(q)
            hidden = 0.2 * q + 0.8 * soft
            logit = logit + jnp.sum(disc_ref[4] * hidden, keepdims=True)
            dq = (disc_ref[4] / PIX) * (0.2 + 0.8 * sig)
            chunks.append(
                [jnp.sum(disc_ref[ch] * dq, axis=0, keepdims=True) for ch in range(3)]
            )
        logit = logit / PIX
        e = jnp.exp(-jnp.abs(logit))
        g = -jnp.where(logit >= 0.0, e, 1.0) / (1.0 + e)
        rows = [jnp.concatenate([c[ch] for c in chunks], axis=1) * g for ch in range(3)]
        out_rows.append(jnp.concatenate(rows + [jnp.zeros((5, PIX), f32)], axis=0))
        wide = jnp.broadcast_to(logit, (1, lanes))
        hi = wide.astype(bf16).astype(f32)
        mid = (wide - hi).astype(bf16).astype(f32)
        logits += [hi, mid, wide - hi - mid]
    dimage = jnp.concatenate(out_rows, axis=1)
    pieces = [
        dimage[ch : ch + 1, n * lanes : (n + 1) * lanes] for ch in range(3) for n in range(count * per)
    ]
    high = jnp.concatenate(pieces, axis=0)
    low = high - high.astype(bf16).astype(f32)
    spare = TAIL - 2 * len(pieces) - len(logits)
    tail_ref[...] = jnp.concatenate(
        [high, low] + logits + [jnp.zeros((spare, lanes), f32)], axis=0
    ).astype(bf16)
    da = head_grad(dimage, rgb_ref) * slope_ref[...]
    store_gz(da, z_ref[...], demod_ref, pay_ref)

    def put(d, b, block):
        at = (d // 2) * count * PIX + b * PIX
        if d % 2 == 0:
            keep_ref[at : at + PIX, :] = block
        else:
            send_ref[at : at + PIX, :] = block.astype(bf16)

    store_dx(pay_ref[: count * PIX, :], wslot_ref, stys_ref, put)


def pair_kernel(keep_ref, got_ref, tail_ref, near_ref, far_ref):
    rows = far_ref.shape[0]
    near_ref[rows:, :] = tail_ref[...]
    near_ref[:rows, :] = (keep_ref[:rows] + got_ref[:rows].astype(f32)).astype(bf16)
    far_ref[...] = (keep_ref[rows:] + got_ref[rows:].astype(f32)).astype(bf16)


def first_grad_kernel(
    idx, s0_ref, s1_ref, rgb_ref, slope_ref, z_ref, demod_ref, other_ref, tail_ref,
    pay_ref, logit_ref,
):
    count = demod_ref.shape[0]
    pixels = count * PIX
    chunks = pixels // 128

    def put_logits(tail):
        for b in range(count):
            at = 6 * chunks + 3 * b
            logit_ref[b] = jnp.max((tail[at : at + 1] + tail[at + 1 : at + 2]) + tail[at + 2 : at + 3])

    @pl.when(idx[0] == 0)
    def _():
        dx = (s0_ref[:pixels, :].astype(f32) + s1_ref[...].astype(f32)).astype(bf16)
        tail = s0_ref[pixels:, :].astype(f32)
        put_logits(tail)
        both = tail[: 3 * chunks] + tail[3 * chunks : 6 * chunks]
        rows = [
            jnp.concatenate(
                [both[ch * chunks + n : ch * chunks + n + 1] for n in range(chunks)], axis=1
            )
            for ch in range(3)
        ]
        dimage = jnp.concatenate(rows + [jnp.zeros((5, pixels), f32)], axis=0)
        da = (head_grad(dimage, rgb_ref) + dx.astype(f32)) * slope_ref[...]
        store_gz(da, z_ref[...], demod_ref, pay_ref)

    @pl.when(idx[0] != 0)
    def _():
        put_logits(tail_ref[...].astype(f32))
        pay_ref[...] = other_ref[...]


def share_kernel(pay_ref, wslot_ref, stys_ref, *out_refs):
    pixels = stys_ref.shape[0] * PIX

    def put(d, b, block):
        out_refs[d][b * PIX : (b + 1) * PIX, :] = block.astype(bf16)

    store_dx(pay_ref[:pixels, :], wslot_ref, stys_ref, put)


def turn_kernel(idx, xa_ref, xb_ref, sty_ref, out_ref, half_ref):
    chan = idx[1]
    full = xa_ref.shape[1]
    count = sty_ref.shape[0]
    own = full // 4

    def turn(ref):
        for d in range(4):
            start = pl.multiple_of((chan ^ d) * own, own)
            out_ref[pl.ds(start, own), :] = ref[:, d * own : (d + 1) * own].T

    @pl.when(idx[0] == 0)
    def _():
        turn(xa_ref)

    @pl.when(idx[0] != 0)
    def _():
        turn(xb_ref)

    sty = sty_ref[...]
    hi = sty.astype(bf16).astype(f32)
    mid = (sty - hi).astype(bf16).astype(f32)
    lo = sty - hi - mid
    rows = [hi, mid, lo]
    tail = jnp.concatenate(
        rows + [jnp.zeros((EXTRA - 3 * count, full), f32)], axis=0
    ).astype(bf16)
    out_ref[full:, :] = tail
    half = full // 2
    start = pl.multiple_of((chan & 1) * half, half)
    half_ref[:half, :] = out_ref[pl.ds(start, half), :]
    half_ref[half:, :] = tail


def taps_of(pay_ref, y, g_ref):
    own = pay_ref.shape[1]
    pixels = pay_ref.shape[0] - EXTRA
    count = pixels // PIX
    stride = PIX + 2 * RES
    zeros = jnp.zeros((RES, own), bf16)
    gz = pay_ref[:pixels, :].astype(f32)
    for kx in range(3):
        moved = col_shift(gz, 1 - kx).astype(bf16)
        for b in range(count):
            at = b * stride
            g_ref[kx, at : at + RES, :] = zeros
            g_ref[kx, at + RES : at + RES + PIX, :] = moved[b * PIX : (b + 1) * PIX]
            g_ref[kx, at + RES + PIX : at + stride, :] = zeros
    taps = []
    for j in range(3):
        k = 2 * y + j
        ky = k // 3
        kx = k - 3 * ky
        rows = []
        for b in range(count):
            start = b * stride + (2 - ky) * RES
            rows.append(g_ref[kx, pl.ds(pl.multiple_of(start, RES), PIX), :])
        taps.append(jnp.concatenate(rows, axis=0))
    return jnp.concatenate(taps, axis=1)


def own_weight_kernel(idx, pay_ref, own_ref, acc_ref, g_ref):
    full = own_ref.shape[0] - EXTRA
    acc_ref[...] = jnp.dot(
        own_ref[:full, :], taps_of(pay_ref, idx[2], g_ref), preferred_element_type=f32
    )


def weight_kernel(idx, *refs):
    pays, own_ref, near, far, w_ref, first_ref = refs[:4], refs[4], refs[5:8], refs[8:11], refs[11], refs[12]
    keep_ref, send_ref = refs[13:15]
    g_ref, acc_ref, sum_ref = refs[15:18]
    core, y, z = idx[1] & 1, idx[2], idx[3]
    full = own_ref.shape[0] - EXTRA
    half = full // 2
    own = pays[0].shape[1]
    pixels = pays[0].shape[0] - EXTRA
    count = pixels // PIX
    rest = [taps_of(pays[n], y, g_ref.at[n - 1]) for n in (1, 2, 3)]
    for refs_, where in ((near, core), (far, 1 - core)):
        part = None
        for ref, taps in zip(refs_, rest):
            more = jnp.dot(ref[:half, :], taps, preferred_element_type=f32)
            part = more if part is None else part + more
        at = pl.ds(pl.multiple_of(where * half, half), half)
        acc_ref[at, :] = first_ref[at, :] + part
    sty_rows, coef_rows = [], []
    for n in range(4):
        tail = own_ref[full:, :] if n == 0 else near[n - 1][half:, :]
        tail = tail.astype(f32)
        sty = tail[:count] + tail[count : 2 * count] + tail[2 * count : 3 * count]
        sty_rows.append(sty * sty)
        tail = pays[n][pixels:, :].astype(f32)
        coef_rows.append(tail[:count] + tail[8 : 8 + count])
    left = pad_rows(jnp.concatenate(sty_rows, axis=0), own).T
    right = pad_rows(jnp.concatenate(coef_rows, axis=0), own)
    demod_term = jnp.dot(left, right, precision=lax.Precision.HIGHEST, preferred_element_type=f32)
    for j in range(3):
        start = pl.multiple_of((2 * y + j) * full, full)
        w = w_ref[pl.ds(start, full), :].astype(f32)
        sum_ref[j * full : (j + 1) * full, :] = (
            acc_ref[:, j * own : (j + 1) * own] + w * demod_term
        )
    rows = keep_ref.shape[0] // 4
    for e in range(4):
        for ref, first in ((keep_ref, z), (send_ref, z ^ 1)):
            start = y * own + ((first + 2 * e) & 7) * rows
            block = sum_ref[pl.ds(pl.multiple_of(start, RES), rows), :]
            ref[e * rows : (e + 1) * rows, :] = block.astype(ref.dtype)


def z_pair_kernel(keep_ref, got_ref, own_ref, *out_refs):
    rows = own_ref.shape[0]
    own_ref[...] = keep_ref[:rows] + got_ref[:rows].astype(f32)
    for e, ref in enumerate(out_refs):
        at = slice((e + 1) * rows, (e + 2) * rows)
        ref[...] = (keep_ref[at] + got_ref[at].astype(f32)).astype(bf16)


def total_kernel(count, *refs):
    grad_ref, dx_ref = refs[-2:]
    total = refs[0][...].astype(f32)
    for ref in refs[1:count]:
        total = total + ref[...].astype(f32)
    grad_ref[...] = total
    shares = [ref[...].astype(f32) for ref in refs[count : count + 4]]
    dx = ((shares[0] + shares[1]) + (shares[2] + shares[3])).astype(bf16)
    for b in range(dx_ref.shape[0]):
        dx_ref[b] = dx[b * PIX : (b + 1) * PIX].T


def call(kernel, outs, args, scratch=(), scalars=0, raws=0, keep=True):
    smem = pl.BlockSpec(memory_space=pltpu.SMEM)
    vmem = pl.BlockSpec(memory_space=pltpu.VMEM)
    plain = scalars + raws
    args = (
        list(args[:scalars])
        + [pltpu.with_memory_space_constraint(a, pltpu.HBM) for a in args[scalars:plain]]
        + [pltpu.with_memory_space_constraint(a, pltpu.VMEM) for a in args[plain:]]
    )
    hbm = pl.BlockSpec(memory_space=pltpu.HBM)
    place = pltpu.VMEM if keep else jax.ShapeDtypeStruct
    return pl.pallas_call(
        kernel,
        out_shape=[
            jax.ShapeDtypeStruct(*o[:2]) if len(o) > 2 else place(*o) for o in outs
        ],
        in_specs=[smem] * scalars + [hbm] * raws + [vmem] * (len(args) - plain),
        out_specs=[smem if len(o) > 2 else vmem for o in outs],
        scratch_shapes=list(scratch),
        compiler_params=pltpu.CompilerParams(vmem_limit_bytes=20 * 2**20),
    )(*args)


def body(
    base, style, noise, conv_weight, conv_bias, noise_gain, rgb_weight, disc_weight, disc_bias,
    disc_out,
):
    weight, styles, noises, rgb = conv_weight[0], style[0], noise[0], rgb_weight[0]
    own = weight.shape[1]
    full = weight.shape[0] // TAPS
    count = base.shape[0]
    pixels = count * PIX
    dp_index = lax.axis_index("dp")
    idx = jnp.stack(
        [lax.axis_index("segment"), lax.axis_index("chan"), dp_index // 8, dp_index % 8]
    ).astype(jnp.int32)

    def across(value, links):
        return lax.ppermute(value, ("segment", "chan"), links)

    def over_y(value, d):
        return lax.ppermute(
            value, "dp", [(y * 8 + z, (y + d) % 4 * 8 + z) for y in range(4) for z in range(8)]
        )

    def over_z(value, d):
        return lax.ppermute(
            value, "dp", [(y * 8 + z, y * 8 + (z + d) % 8) for y in range(4) for z in range(8)]
        )

    def flip(value, d):
        return across(value, [(s * 4 + c, (1 - s) * 4 + (c ^ d)) for s in range(2) for c in range(4)])

    def within(value, d):
        return across(value, [(s * 4 + c, s * 4 + (c ^ d)) for s in range(2) for c in range(4)])

    x2 = flip(base, 2)
    x1 = within(base, 1)
    x3 = within(x2, 1)
    sources = [
        weight, styles, noises, noise_gain, conv_bias, disc_weight, disc_bias[None], disc_out[None],
        rgb,
    ]
    wslot, stys, demod, nb, disc, rgbp, sty = call(
        prep_kernel,
        [
            ((full, TAPS * own), bf16),
            ((count, full), f32),
            ((count, own), f32),
            ((pixels, own), f32),
            ((5, disc_weight.shape[1], own), f32),
            ((EXTRA, own), bf16),
            ((count, full), f32),
        ],
        [idx, *sources],
        scratch=[pltpu.VMEM(a.shape, a.dtype) for a in sources]
        + [pltpu.SemaphoreType.DMA((len(sources),))],
        scalars=1,
        raws=len(sources),
    )
    conv_outs = [
        ((pixels + EXTRA, own), bf16),
        ((pixels, own), f32),
        ((pixels, own), f32),
        ((pixels, full), bf16),
    ]
    pay, slope_a, z_a, xm_a = call(
        functools.partial(conv_kernel, False),
        conv_outs,
        [base, x1, x2, x3, stys, wslot, demod, nb, rgbp],
    )
    y0 = flip(pay, 0)
    y2 = flip(pay, 2)
    y1 = within(y0, 1)
    y3 = within(y2, 1)
    _, slope_b, z_b, xm_b, image_own = call(
        functools.partial(conv_kernel, True),
        conv_outs + [((8, pixels), f32)],
        [y0, y1, y2, y3, stys, wslot, demod, nb, rgbp],
    )
    images = [within(image_own, d) for d in (1, 2, 3)]
    xm, xm_half = call(
        turn_kernel,
        [((full + EXTRA, pixels), bf16), ((full // 2 + EXTRA, pixels), bf16)],
        [idx, xm_a, xm_b, sty],
        scalars=1,
    )
    (image_first,) = call(first_image_kernel, [((8, pixels), f32)], [y0, y1, y2, y3])
    near = [over_y(xm_half, d) for d in (1, 2, 3)]
    far = [within(near[n], 1) for n in range(3)]
    two = (2 * pixels, own)
    tail, pay_b, dx_keep, dx_send = call(
        disc_kernel,
        [((TAIL, own), bf16), ((pixels + EXTRA, own), bf16), (two, f32), (two, bf16)],
        [image_own, *images, image_first, disc, rgbp, slope_b, z_b, demod, wslot, stys],
    )
    dx_got = within(dx_send, 1)
    share = ((pixels, own), bf16)
    dx_near, dx_far = call(
        pair_kernel, [((pixels + TAIL, own), bf16), share], [dx_keep, dx_got, tail]
    )
    got = [flip(dx_near, 0), flip(dx_far, 2)]
    pay_g, logits = call(
        first_grad_kernel,
        [((pixels + EXTRA, own), bf16), ((count,), f32, True)],
        [idx, *got, rgbp, slope_a, z_a, demod, pay_b, tail],
        scalars=1,
    )
    pays = [pay_g] + [over_y(pay_g, d) for d in (1, 2, 3)]
    shares = call(share_kernel, [share] * 4, [pay_g, wslot, stys])
    mine = [shares[0]] + [within(shares[d], d) for d in (1, 2, 3)]
    rows = weight.shape[0] // 32
    taps = (3, count * (PIX + 2 * RES), own)
    (first,) = call(
        own_weight_kernel,
        [((full, 3 * own), f32)],
        [idx, pay_g, xm],
        scratch=[pltpu.VMEM(taps, bf16)],
        scalars=1,
    )
    z_keep, z_send = call(
        weight_kernel,
        [((4 * rows, own), f32), ((4 * rows, own), bf16)],
        [idx, *pays, xm, *near, *far, weight, first],
        scratch=[
            pltpu.VMEM((3, *taps), bf16),
            pltpu.VMEM((full, 3 * own), f32),
            pltpu.VMEM((3 * full, own), f32),
        ],
        scalars=1,
    )
    z_got = lax.ppermute(z_send, "dp", [(n, n ^ 1) for n in range(32)])
    block = (rows, own)
    z_own, *z_outs = call(z_pair_kernel, [(block, f32)] + [(block, bf16)] * 3, [z_keep, z_got])
    parts = [z_own] + [over_z(z_outs[e - 1], 2 * e) for e in (1, 2, 3)]
    grad_rows, dx = call(
        functools.partial(total_kernel, len(parts)),
        [((rows, own), f32), ((count, own, PIX), bf16)],
        [*parts, *mine],
        keep=False,
    )
    return (grad_rows[None], logits, dx[None])


def solution(mesh):
    placed = (
        P("dp", "chan", None),
        P("segment", "dp", None),
        P("segment", "dp", None),
        P("segment", None, "chan"),
        P("segment", "chan"),
        P("segment", "chan"),
        P("segment", None, "chan"),
        P(),
        P(),
        P(),
    )
    return jax.shard_map(
        body,
        mesh=mesh,
        in_specs=placed,
        out_specs=(P("segment", "dp", "chan"), P("dp"), P("segment", "dp", "chan", None)),
        check_vma=False,
    )
```

```python
import functools

import jax
import jax.numpy as jnp
from jax import lax
from jax.experimental import pallas as pl
from jax.experimental.pallas import tpu as pltpu
from jax.sharding import PartitionSpec as P


RES = 16
PIX = RES * RES
TAPS = 9
EXTRA = 16
TAIL = 32
epsilon = 1e-06
root_two = 1.4142135623730951
f32 = jnp.float32
bf16 = jnp.bfloat16


NT = (((1,), (1,)), ((), ()))


def act_parts(t):
    e = jnp.exp(-jnp.abs(t))
    r = 1.0 / (1.0 + e)
    soft = jnp.maximum(t, 0.0) + jnp.log(1.0 + e)
    sig = jnp.where(t >= 0.0, r, e * r)
    return soft, sig


def row_shift(v, a):
    if a == 0:
        return v
    zeros = jnp.zeros((RES, v.shape[1]), v.dtype)
    parts = []
    for b in range(v.shape[0] // PIX):
        base = b * PIX
        if a > 0:
            parts += [v[base + RES : base + PIX], zeros]
        else:
            parts += [zeros, v[base : base + PIX - RES]]
    return jnp.concatenate(parts, axis=0)


def col_shift(v, b):
    if b == 0:
        return v
    x = lax.broadcasted_iota(jnp.int32, v.shape, 0) & (RES - 1)
    if b > 0:
        return jnp.where(x < RES - 1, pltpu.roll(v, v.shape[0] - 1, 0), 0.0)
    return jnp.where(x > 0, pltpu.roll(v, 1, 0), 0.0)


def pad_rows(v, rows):
    return jnp.concatenate([v, jnp.zeros((rows - v.shape[0], v.shape[1]), v.dtype)], axis=0)


def prep_kernel(idx, *refs):
    number = (len(refs) - 8) // 2
    sources, outs, copies = refs[:number], refs[number : number + 7], refs[number + 7 : -1]
    sem = refs[-1]
    moves = [
        pltpu.make_async_copy(src, dst, sem.at[n]) for n, (src, dst) in enumerate(zip(sources, copies))
    ]
    for move in moves:
        move.start()
    for move in moves:
        move.wait()
    w_ref, sty_ref, noise_ref, gain_ref, bias_ref, dw_ref, db_ref, do_ref, rgb_ref = copies
    wslot_ref, stys_ref, demod_ref, nb_ref, disc_ref, rgbp_ref, stycopy_ref = outs
    rgbp_ref[...] = pad_rows(rgb_ref[...], EXTRA)
    stycopy_ref[...] = sty_ref[...]
    chan = idx[1]
    own = w_ref.shape[1]
    full = w_ref.shape[0] // TAPS
    count = sty_ref.shape[0]
    chans = full // own
    for d in range(chans):
        part = chan ^ d
        for k in range(TAPS):
            start = pl.multiple_of(k * full + part * own, own)
            wslot_ref[d * own : (d + 1) * own, k * own : (k + 1) * own] = w_ref[pl.ds(start, own), :]
        stys_ref[:, d * own : (d + 1) * own] = sty_ref[:, pl.ds(pl.multiple_of(part * own, own), own)]
    squares = jnp.zeros((full, own), f32)
    for k in range(TAPS):
        w = w_ref[k * full : (k + 1) * full, :].astype(f32)
        squares = squares + w * w
    sty = sty_ref[...]
    cols = pad_rows(sty * sty, own).T
    for b in range(count):
        total = jnp.sum(cols[:, b : b + 1] * squares, axis=0, keepdims=True)
        demod_ref[b : b + 1, :] = lax.rsqrt(total + epsilon)
        noise = jnp.broadcast_to(noise_ref[b : b + 1, :], (own, PIX)).T
        nb_ref[b * PIX : (b + 1) * PIX, :] = gain_ref[...] * noise + bias_ref[...]
    rows = [dw_ref[0:1, :], dw_ref[1:2, :], dw_ref[2:3, :], db_ref[...], do_ref[...]]
    for n, row in enumerate(rows):
        disc_ref[n] = jnp.broadcast_to(row, (own, row.shape[1])).T


def conv_kernel(second, *refs):
    x_refs = refs[:4]
    stys_ref, wslot_ref, demod_ref, nb_ref, rgb_ref = refs[4:9]
    pay_ref, slope_ref, z_ref, xm_ref = refs[9:13]
    count = stys_ref.shape[0]
    own = demod_ref.shape[1]
    pixels = count * PIX
    for d in range(4):
        for b in range(count):
            sty = stys_ref[b : b + 1, d * own : (d + 1) * own]
            x = x_refs[d][b * PIX : (b + 1) * PIX, :] if second else x_refs[d][b].T
            x = x.astype(f32)
            xm_ref[b * PIX : (b + 1) * PIX, d * own : (d + 1) * own] = (x * sty).astype(bf16)
    products = jnp.dot(xm_ref[...], wslot_ref[...], preferred_element_type=f32)
    z = None
    for kx in range(3):
        total = None
        for ky in range(3):
            k = 3 * ky + kx
            moved = row_shift(products[:, k * own : (k + 1) * own], ky - 1)
            total = moved if total is None else total + moved
        total = col_shift(total, kx - 1)
        z = total if z is None else z + total
    z_ref[...] = z
    demod = jnp.concatenate(
        [jnp.broadcast_to(demod_ref[b : b + 1, :], (PIX, own)) for b in range(count)], axis=0
    )
    pre = demod * z + nb_ref[...]
    soft, sig = act_parts(pre)
    y = (root_two * (0.2 * pre + 0.8 * soft)).astype(bf16)
    slope_ref[...] = root_two * (0.2 + 0.8 * sig)
    rgb = rgb_ref[...]
    pay_ref[:pixels, :] = y
    pay_ref[pixels:, :] = rgb
    if second:
        refs[13][...] = lax.dot_general(rgb, y, NT, preferred_element_type=f32)[:8]


def first_image_kernel(*refs):
    out_ref = refs[-1]
    pixels = out_ref.shape[1]
    parts = [
        lax.dot_general(ref[pixels:, :], ref[:pixels, :], NT, preferred_element_type=f32)[:8]
        for ref in refs[:4]
    ]
    out_ref[...] = (parts[0] + parts[1]) + (parts[2] + parts[3])


def head_grad(dimage, rgb_ref):
    own = rgb_ref.shape[1]
    hi = dimage.astype(bf16).astype(f32)
    lo = dimage - hi
    left = pad_rows(jnp.concatenate([hi, lo], axis=0), own).T.astype(bf16)
    rgb = rgb_ref[...].astype(f32)[:8]
    right = jnp.concatenate([rgb, rgb], axis=0)
    return jnp.dot(left, pad_rows(right, own).astype(bf16), preferred_element_type=f32)


def store_gz(da, z, demod_ref, pay_ref):
    count, own = demod_ref.shape
    rows = []
    for b in range(count):
        demod = demod_ref[b : b + 1, :]
        part = da[b * PIX : (b + 1) * PIX]
        pay_ref[b * PIX : (b + 1) * PIX, :] = (part * demod).astype(bf16)
        d_demod = jnp.sum(part * z[b * PIX : (b + 1) * PIX], axis=0, keepdims=True)
        rows.append(-d_demod * demod * demod * demod)
    coef = jnp.concatenate(rows + [jnp.zeros((8 - count, own), f32)], axis=0)
    hi = coef.astype(bf16).astype(f32)
    pay_ref[count * PIX :, :] = jnp.concatenate([hi, coef - hi], axis=0).astype(bf16)


def store_dx(gz, wslot_ref, stys_ref, put):
    count = stys_ref.shape[0]
    own = gz.shape[1]
    gz = gz.astype(f32)
    by_col = [col_shift(gz, 1 - kx).astype(bf16) for kx in range(3)]
    cols = jnp.concatenate(
        [row_shift(by_col[k % 3], 1 - k // 3) for k in range(TAPS)], axis=1
    )
    share = lax.dot_general(cols, wslot_ref[...], NT, preferred_element_type=f32)
    for d in range(4):
        for b in range(count):
            sty = stys_ref[b : b + 1, d * own : (d + 1) * own]
            put(d, b, share[b * PIX : (b + 1) * PIX, d * own : (d + 1) * own] * sty)


def disc_kernel(
    own_ref, r1_ref, r2_ref, r3_ref, first_ref, disc_ref, rgb_ref, slope_ref, z_ref, demod_ref,
    wslot_ref, stys_ref, tail_ref, pay_ref, keep_ref, send_ref,
):
    image = ((own_ref[...] + r1_ref[...]) + (r2_ref[...] + r3_ref[...])) + first_ref[...]
    lanes = 128
    per = PIX // lanes
    count = stys_ref.shape[0]
    out_rows, logits = [], []
    for b in range(count):
        logit = jnp.zeros((1, 1), f32)
        chunks = []
        for n in range(per):
            at = b * PIX + n * lanes
            q = disc_ref[3]
            for ch in range(3):
                q = q + disc_ref[ch] * image[ch : ch + 1, at : at + lanes]
            soft, sig = act_parts(q)
            hidden = 0.2 * q + 0.8 * soft
            logit = logit + jnp.sum(disc_ref[4] * hidden, keepdims=True)
            dq = (disc_ref[4] / PIX) * (0.2 + 0.8 * sig)
            chunks.append(
                [jnp.sum(disc_ref[ch] * dq, axis=0, keepdims=True) for ch in range(3)]
            )
        logit = logit / PIX
        e = jnp.exp(-jnp.abs(logit))
        g = -jnp.where(logit >= 0.0, e, 1.0) / (1.0 + e)
        rows = [jnp.concatenate([c[ch] for c in chunks], axis=1) * g for ch in range(3)]
        out_rows.append(jnp.concatenate(rows + [jnp.zeros((5, PIX), f32)], axis=0))
        wide = jnp.broadcast_to(logit, (1, lanes))
        hi = wide.astype(bf16).astype(f32)
        mid = (wide - hi).astype(bf16).astype(f32)
        logits += [hi, mid, wide - hi - mid]
    dimage = jnp.concatenate(out_rows, axis=1)
    pieces = [
        dimage[ch : ch + 1, n * lanes : (n + 1) * lanes] for ch in range(3) for n in range(count * per)
    ]
    high = jnp.concatenate(pieces, axis=0)
    low = high - high.astype(bf16).astype(f32)
    spare = TAIL - 2 * len(pieces) - len(logits)
    tail_ref[...] = jnp.concatenate(
        [high, low] + logits + [jnp.zeros((spare, lanes), f32)], axis=0
    ).astype(bf16)
    da = head_grad(dimage, rgb_ref) * slope_ref[...]
    store_gz(da, z_ref[...], demod_ref, pay_ref)

    def put(d, b, block):
        at = (d // 2) * count * PIX + b * PIX
        if d % 2 == 0:
            keep_ref[at : at + PIX, :] = block
        else:
            send_ref[at : at + PIX, :] = block.astype(bf16)

    store_dx(pay_ref[: count * PIX, :], wslot_ref, stys_ref, put)


def pair_kernel(keep_ref, got_ref, tail_ref, near_ref, far_ref):
    rows = far_ref.shape[0]
    near_ref[rows:, :] = tail_ref[...]
    near_ref[:rows, :] = (keep_ref[:rows] + got_ref[:rows].astype(f32)).astype(bf16)
    far_ref[...] = (keep_ref[rows:] + got_ref[rows:].astype(f32)).astype(bf16)


def first_grad_kernel(
    idx, s0_ref, s1_ref, rgb_ref, slope_ref, z_ref, demod_ref, other_ref, tail_ref,
    pay_ref, logit_ref,
):
    count = demod_ref.shape[0]
    pixels = count * PIX
    chunks = pixels // 128

    def put_logits(tail):
        for b in range(count):
            at = 6 * chunks + 3 * b
            logit_ref[b] = jnp.max((tail[at : at + 1] + tail[at + 1 : at + 2]) + tail[at + 2 : at + 3])

    @pl.when(idx[0] == 0)
    def _():
        dx = (s0_ref[:pixels, :].astype(f32) + s1_ref[...].astype(f32)).astype(bf16)
        tail = s0_ref[pixels:, :].astype(f32)
        put_logits(tail)
        both = tail[: 3 * chunks] + tail[3 * chunks : 6 * chunks]
        rows = [
            jnp.concatenate(
                [both[ch * chunks + n : ch * chunks + n + 1] for n in range(chunks)], axis=1
            )
            for ch in range(3)
        ]
        dimage = jnp.concatenate(rows + [jnp.zeros((5, pixels), f32)], axis=0)
        da = (head_grad(dimage, rgb_ref) + dx.astype(f32)) * slope_ref[...]
        store_gz(da, z_ref[...], demod_ref, pay_ref)

    @pl.when(idx[0] != 0)
    def _():
        put_logits(tail_ref[...].astype(f32))
        pay_ref[...] = other_ref[...]


def share_kernel(pay_ref, wslot_ref, stys_ref, *out_refs):
    pixels = stys_ref.shape[0] * PIX

    def put(d, b, block):
        out_refs[d][b * PIX : (b + 1) * PIX, :] = block.astype(bf16)

    store_dx(pay_ref[:pixels, :], wslot_ref, stys_ref, put)


def turn_kernel(idx, xa_ref, xb_ref, sty_ref, out_ref, half_ref):
    chan = idx[1]
    full = xa_ref.shape[1]
    count = sty_ref.shape[0]
    own = full // 4

    def turn(ref):
        for d in range(4):
            start = pl.multiple_of((chan ^ d) * own, own)
            out_ref[pl.ds(start, own), :] = ref[:, d * own : (d + 1) * own].T

    @pl.when(idx[0] == 0)
    def _():
        turn(xa_ref)

    @pl.when(idx[0] != 0)
    def _():
        turn(xb_ref)

    sty = sty_ref[...]
    hi = sty.astype(bf16).astype(f32)
    mid = (sty - hi).astype(bf16).astype(f32)
    lo = sty - hi - mid
    rows = [hi, mid, lo]
    tail = jnp.concatenate(
        rows + [jnp.zeros((EXTRA - 3 * count, full), f32)], axis=0
    ).astype(bf16)
    out_ref[full:, :] = tail
    half = full // 2
    start = pl.multiple_of((chan & 1) * half, half)
    half_ref[:half, :] = out_ref[pl.ds(start, half), :]
    half_ref[half:, :] = tail


def taps_of(pay_ref, y, g_ref):
    own = pay_ref.shape[1]
    pixels = pay_ref.shape[0] - EXTRA
    count = pixels // PIX
    stride = PIX + 2 * RES
    zeros = jnp.zeros((RES, own), bf16)
    gz = pay_ref[:pixels, :].astype(f32)
    for kx in range(3):
        moved = col_shift(gz, 1 - kx).astype(bf16)
        for b in range(count):
            at = b * stride
            g_ref[kx, at : at + RES, :] = zeros
            g_ref[kx, at + RES : at + RES + PIX, :] = moved[b * PIX : (b + 1) * PIX]
            g_ref[kx, at + RES + PIX : at + stride, :] = zeros
    taps = []
    for j in range(3):
        k = 2 * y + j
        ky = k // 3
        kx = k - 3 * ky
        rows = []
        for b in range(count):
            start = b * stride + (2 - ky) * RES
            rows.append(g_ref[kx, pl.ds(pl.multiple_of(start, RES), PIX), :])
        taps.append(jnp.concatenate(rows, axis=0))
    return jnp.concatenate(taps, axis=1)


def own_weight_kernel(idx, pay_ref, own_ref, acc_ref, g_ref):
    full = own_ref.shape[0] - EXTRA
    acc_ref[...] = jnp.dot(
        own_ref[:full, :], taps_of(pay_ref, idx[2], g_ref), preferred_element_type=f32
    )


def add_half_rows(taps, near, far, core, before_ref, after_ref):
    half = near[0].shape[0] - EXTRA
    for group, where in ((near, core), (far, 1 - core)):
        part = None
        for ref, tap in zip(group, taps):
            more = jnp.dot(ref[:half, :], tap, preferred_element_type=f32)
            part = more if part is None else part + more
        at = pl.ds(pl.multiple_of(where * half, half), half)
        after_ref[at, :] = before_ref[at, :] + part


def near_weight_kernel(idx, p1_ref, p3_ref, n1_ref, n3_ref, f1_ref, f3_ref, before_ref, acc_ref, g_ref):
    taps = [taps_of(ref, idx[2], g_ref.at[n]) for n, ref in enumerate((p1_ref, p3_ref))]
    add_half_rows(taps, (n1_ref, n3_ref), (f1_ref, f3_ref), idx[1] & 1, before_ref, acc_ref)


def weight_kernel(idx, *refs):
    pays, own_ref, near, far_ref, w_ref, before_ref = refs[:4], refs[4], refs[5:8], refs[8], refs[9], refs[10]
    keep_ref, send_ref = refs[11:13]
    g_ref, acc_ref, sum_ref = refs[13:16]
    core, y, z = idx[1] & 1, idx[2], idx[3]
    full = own_ref.shape[0] - EXTRA
    half = full // 2
    own = pays[0].shape[1]
    pixels = pays[0].shape[0] - EXTRA
    count = pixels // PIX
    taps = taps_of(pays[2], y, g_ref)
    add_half_rows((taps,), (near[1],), (far_ref,), core, before_ref, acc_ref)
    sty_rows, coef_rows = [], []
    for n in range(4):
        tail = own_ref[full:, :] if n == 0 else near[n - 1][half:, :]
        tail = tail.astype(f32)
        sty = tail[:count] + tail[count : 2 * count] + tail[2 * count : 3 * count]
        sty_rows.append(sty * sty)
        tail = pays[n][pixels:, :].astype(f32)
        coef_rows.append(tail[:count] + tail[8 : 8 + count])
    left = pad_rows(jnp.concatenate(sty_rows, axis=0), own).T
    right = pad_rows(jnp.concatenate(coef_rows, axis=0), own)
    demod_term = jnp.dot(left, right, precision=lax.Precision.HIGHEST, preferred_element_type=f32)
    for j in range(3):
        start = pl.multiple_of((2 * y + j) * full, full)
        w = w_ref[pl.ds(start, full), :].astype(f32)
        sum_ref[j * full : (j + 1) * full, :] = (
            acc_ref[:, j * own : (j + 1) * own] + w * demod_term
        )
    rows = keep_ref.shape[0] // 4
    for e in range(4):
        for ref, first in ((keep_ref, z), (send_ref, ((z + core) ^ 1) - core)):
            start = y * own + ((first + 2 * e) & 7) * rows
            block = sum_ref[pl.ds(pl.multiple_of(start, RES), rows), :]
            ref[e * rows : (e + 1) * rows, :] = block.astype(ref.dtype)


def z_pair_kernel(keep_ref, got_ref, own_ref, *out_refs):
    rows = own_ref.shape[0]
    own_ref[...] = keep_ref[:rows] + got_ref[:rows].astype(f32)
    for e, ref in enumerate(out_refs):
        at = slice((e + 1) * rows, (e + 2) * rows)
        ref[...] = (keep_ref[at] + got_ref[at].astype(f32)).astype(bf16)


def total_kernel(count, *refs):
    grad_ref, dx_ref = refs[-2:]
    total = refs[0][...].astype(f32)
    for ref in refs[1:count]:
        total = total + ref[...].astype(f32)
    grad_ref[...] = total
    shares = [ref[...].astype(f32) for ref in refs[count : count + 4]]
    dx = ((shares[0] + shares[1]) + (shares[2] + shares[3])).astype(bf16)
    for b in range(dx_ref.shape[0]):
        dx_ref[b] = dx[b * PIX : (b + 1) * PIX].T


def call(kernel, outs, args, scratch=(), scalars=0, raws=0, keep=True):
    smem = pl.BlockSpec(memory_space=pltpu.SMEM)
    vmem = pl.BlockSpec(memory_space=pltpu.VMEM)
    plain = scalars + raws
    args = (
        list(args[:scalars])
        + [pltpu.with_memory_space_constraint(a, pltpu.HBM) for a in args[scalars:plain]]
        + [pltpu.with_memory_space_constraint(a, pltpu.VMEM) for a in args[plain:]]
    )
    hbm = pl.BlockSpec(memory_space=pltpu.HBM)
    place = pltpu.VMEM if keep else jax.ShapeDtypeStruct
    return pl.pallas_call(
        kernel,
        out_shape=[
            jax.ShapeDtypeStruct(*o[:2]) if len(o) > 2 else place(*o) for o in outs
        ],
        in_specs=[smem] * scalars + [hbm] * raws + [vmem] * (len(args) - plain),
        out_specs=[smem if len(o) > 2 else vmem for o in outs],
        scratch_shapes=list(scratch),
        compiler_params=pltpu.CompilerParams(vmem_limit_bytes=20 * 2**20),
    )(*args)


def body(
    base, style, noise, conv_weight, conv_bias, noise_gain, rgb_weight, disc_weight, disc_bias,
    disc_out,
):
    weight, styles, noises, rgb = conv_weight[0], style[0], noise[0], rgb_weight[0]
    own = weight.shape[1]
    full = weight.shape[0] // TAPS
    count = base.shape[0]
    pixels = count * PIX
    dp_index = lax.axis_index("dp")
    idx = jnp.stack(
        [lax.axis_index("segment"), lax.axis_index("chan"), dp_index // 8, dp_index % 8]
    ).astype(jnp.int32)

    def across(value, links):
        return lax.ppermute(value, ("segment", "chan"), links)

    def by_core(value, place):
        links = []
        for y in range(4):
            for z in range(8):
                for c in range(4):
                    to_y, to_z = place(y, z, c % 2)
                    links.append(((y * 8 + z) * 4 + c, (to_y % 4 * 8 + to_z % 8) * 4 + c))
        return lax.ppermute(value, ("dp", "chan"), links)

    def over_y(value, d):
        return by_core(value, lambda y, z, core: (y - d if core else y + d, z))

    def over_z(value, d):
        return lax.ppermute(
            value, "dp", [(y * 8 + z, y * 8 + (z + d) % 8) for y in range(4) for z in range(8)]
        )

    def flip(value, d):
        return across(value, [(s * 4 + c, (1 - s) * 4 + (c ^ d)) for s in range(2) for c in range(4)])

    def within(value, d):
        return across(value, [(s * 4 + c, s * 4 + (c ^ d)) for s in range(2) for c in range(4)])

    x2 = flip(base, 2)
    x1 = within(base, 1)
    x3 = within(x2, 1)
    sources = [
        weight, styles, noises, noise_gain, conv_bias, disc_weight, disc_bias[None], disc_out[None],
        rgb,
    ]
    wslot, stys, demod, nb, disc, rgbp, sty = call(
        prep_kernel,
        [
            ((full, TAPS * own), bf16),
            ((count, full), f32),
            ((count, own), f32),
            ((pixels, own), f32),
            ((5, disc_weight.shape[1], own), f32),
            ((EXTRA, own), bf16),
            ((count, full), f32),
        ],
        [idx, *sources],
        scratch=[pltpu.VMEM(a.shape, a.dtype) for a in sources]
        + [pltpu.SemaphoreType.DMA((len(sources),))],
        scalars=1,
        raws=len(sources),
    )
    conv_outs = [
        ((pixels + EXTRA, own), bf16),
        ((pixels, own), f32),
        ((pixels, own), f32),
        ((pixels, full), bf16),
    ]
    pay, slope_a, z_a, xm_a = call(
        functools.partial(conv_kernel, False),
        conv_outs,
        [base, x1, x2, x3, stys, wslot, demod, nb, rgbp],
    )
    y0 = flip(pay, 0)
    y2 = flip(pay, 2)
    y1 = within(y0, 1)
    y3 = within(y2, 1)
    _, slope_b, z_b, xm_b, image_own = call(
        functools.partial(conv_kernel, True),
        conv_outs + [((8, pixels), f32)],
        [y0, y1, y2, y3, stys, wslot, demod, nb, rgbp],
    )
    images = [within(image_own, d) for d in (1, 2, 3)]
    xm, xm_half = call(
        turn_kernel,
        [((full + EXTRA, pixels), bf16), ((full // 2 + EXTRA, pixels), bf16)],
        [idx, xm_a, xm_b, sty],
        scalars=1,
    )
    (image_first,) = call(first_image_kernel, [((8, pixels), f32)], [y0, y1, y2, y3])
    near_1 = over_y(xm_half, 1)
    near_3 = over_y(xm_half, 3)
    near_2 = over_y(near_1, 1)
    far_1 = within(near_3, 1)
    far_3 = within(near_1, 1)
    far_2 = within(near_2, 1)
    two = (2 * pixels, own)
    tail, pay_b, dx_keep, dx_send = call(
        disc_kernel,
        [((TAIL, own), bf16), ((pixels + EXTRA, own), bf16), (two, f32), (two, bf16)],
        [image_own, *images, image_first, disc, rgbp, slope_b, z_b, demod, wslot, stys],
    )
    dx_got = within(dx_send, 1)
    share = ((pixels, own), bf16)
    dx_near, dx_far = call(
        pair_kernel, [((pixels + TAIL, own), bf16), share], [dx_keep, dx_got, tail]
    )
    got = [flip(dx_near, 0), flip(dx_far, 2)]
    pay_g, logits = call(
        first_grad_kernel,
        [((pixels + EXTRA, own), bf16), ((count,), f32, True)],
        [idx, *got, rgbp, slope_a, z_a, demod, pay_b, tail],
        scalars=1,
    )
    pay_1 = over_y(pay_g, 1)
    pay_3 = over_y(pay_g, 3)
    pay_2 = over_y(pay_1, 1)
    shares = call(share_kernel, [share] * 4, [pay_g, wslot, stys])
    mine = [shares[0]] + [within(shares[d], d) for d in (1, 2, 3)]
    rows = weight.shape[0] // 32
    taps = (3, count * (PIX + 2 * RES), own)
    (first,) = call(
        own_weight_kernel,
        [((full, 3 * own), f32)],
        [idx, pay_g, xm],
        scratch=[pltpu.VMEM(taps, bf16)],
        scalars=1,
    )
    (second,) = call(
        near_weight_kernel,
        [((full, 3 * own), f32)],
        [idx, pay_1, pay_3, near_1, near_3, far_1, far_3, first],
        scratch=[pltpu.VMEM((2, *taps), bf16)],
        scalars=1,
    )
    z_keep, z_send = call(
        weight_kernel,
        [((4 * rows, own), f32), ((4 * rows, own), bf16)],
        [idx, pay_g, pay_1, pay_2, pay_3, xm, near_1, near_2, near_3, far_2, weight, second],
        scratch=[
            pltpu.VMEM(taps, bf16),
            pltpu.VMEM((full, 3 * own), f32),
            pltpu.VMEM((3 * full, own), f32),
        ],
        scalars=1,
    )
    z_got = by_core(z_send, lambda y, z, core: (y, ((z + core) ^ 1) - core))
    block = (rows, own)
    z_own, *z_outs = call(z_pair_kernel, [(block, f32)] + [(block, bf16)] * 3, [z_keep, z_got])
    parts = [z_own] + [over_z(z_outs[e - 1], 2 * e) for e in (1, 2, 3)]
    grad_rows, dx = call(
        functools.partial(total_kernel, len(parts)),
        [((rows, own), f32), ((count, own, PIX), bf16)],
        [*parts, *mine],
        keep=False,
    )
    return (grad_rows[None], logits, dx[None])


def solution(mesh):
    placed = (
        P("dp", "chan", None),
        P("segment", "dp", None),
        P("segment", "dp", None),
        P("segment", None, "chan"),
        P("segment", "chan"),
        P("segment", "chan"),
        P("segment", None, "chan"),
        P(),
        P(),
        P(),
    )
    return jax.shard_map(
        body,
        mesh=mesh,
        in_specs=placed,
        out_specs=(P("segment", "dp", "chan"), P("dp"), P("segment", "dp", "chan", None)),
        check_vma=False,
    )
```

```python
import functools

import jax
import jax.numpy as jnp
from jax import lax
from jax.experimental import pallas as pl
from jax.experimental.pallas import tpu as pltpu
from jax.sharding import PartitionSpec as P


RES = 16
PIX = RES * RES
TAPS = 9
EXTRA = 16
TAIL = 32
epsilon = 1e-06
root_two = 1.4142135623730951
f32 = jnp.float32
bf16 = jnp.bfloat16


NT = (((1,), (1,)), ((), ()))


def act_parts(t):
    e = jnp.exp(-jnp.abs(t))
    r = 1.0 / (1.0 + e)
    soft = jnp.maximum(t, 0.0) + jnp.log(1.0 + e)
    sig = jnp.where(t >= 0.0, r, e * r)
    return soft, sig


def row_shift(v, a):
    if a == 0:
        return v
    zeros = jnp.zeros((RES, v.shape[1]), v.dtype)
    parts = []
    for b in range(v.shape[0] // PIX):
        base = b * PIX
        if a > 0:
            parts += [v[base + RES : base + PIX], zeros]
        else:
            parts += [zeros, v[base : base + PIX - RES]]
    return jnp.concatenate(parts, axis=0)


def col_shift(v, b):
    if b == 0:
        return v
    x = lax.broadcasted_iota(jnp.int32, v.shape, 0) & (RES - 1)
    if b > 0:
        return jnp.where(x < RES - 1, pltpu.roll(v, v.shape[0] - 1, 0), 0.0)
    return jnp.where(x > 0, pltpu.roll(v, 1, 0), 0.0)


def pad_rows(v, rows):
    return jnp.concatenate([v, jnp.zeros((rows - v.shape[0], v.shape[1]), v.dtype)], axis=0)


def prep_kernel(idx, *refs):
    number = (len(refs) - 8) // 2
    sources, outs, copies = refs[:number], refs[number : number + 7], refs[number + 7 : -1]
    sem = refs[-1]
    moves = [
        pltpu.make_async_copy(src, dst, sem.at[n]) for n, (src, dst) in enumerate(zip(sources, copies))
    ]
    for move in moves:
        move.start()
    for move in moves:
        move.wait()
    w_ref, sty_ref, noise_ref, gain_ref, bias_ref, dw_ref, db_ref, do_ref, rgb_ref = copies
    wslot_ref, stys_ref, demod_ref, nb_ref, disc_ref, rgbp_ref, stycopy_ref = outs
    rgbp_ref[...] = pad_rows(rgb_ref[...], EXTRA)
    stycopy_ref[...] = sty_ref[...]
    chan = idx[1]
    own = w_ref.shape[1]
    full = w_ref.shape[0] // TAPS
    count = sty_ref.shape[0]
    chans = full // own
    for d in range(chans):
        part = chan ^ d
        for k in range(TAPS):
            start = pl.multiple_of(k * full + part * own, own)
            wslot_ref[d * own : (d + 1) * own, k * own : (k + 1) * own] = w_ref[pl.ds(start, own), :]
        stys_ref[:, d * own : (d + 1) * own] = sty_ref[:, pl.ds(pl.multiple_of(part * own, own), own)]
    squares = jnp.zeros((full, own), f32)
    for k in range(TAPS):
        w = w_ref[k * full : (k + 1) * full, :].astype(f32)
        squares = squares + w * w
    sty = sty_ref[...]
    cols = pad_rows(sty * sty, own).T
    for b in range(count):
        total = jnp.sum(cols[:, b : b + 1] * squares, axis=0, keepdims=True)
        demod_ref[b : b + 1, :] = lax.rsqrt(total + epsilon)
        noise = jnp.broadcast_to(noise_ref[b : b + 1, :], (own, PIX)).T
        nb_ref[b * PIX : (b + 1) * PIX, :] = gain_ref[...] * noise + bias_ref[...]
    rows = [dw_ref[0:1, :], dw_ref[1:2, :], dw_ref[2:3, :], db_ref[...], do_ref[...]]
    for n, row in enumerate(rows):
        disc_ref[n] = jnp.broadcast_to(row, (own, row.shape[1])).T


def conv_kernel(second, *refs):
    x_refs = refs[:4]
    stys_ref, wslot_ref, demod_ref, nb_ref, rgb_ref = refs[4:9]
    pay_ref, slope_ref, z_ref, xm_ref = refs[9:13]
    count = stys_ref.shape[0]
    own = demod_ref.shape[1]
    pixels = count * PIX
    for d in range(4):
        for b in range(count):
            sty = stys_ref[b : b + 1, d * own : (d + 1) * own]
            x = x_refs[d][b * PIX : (b + 1) * PIX, :] if second else x_refs[d][b].T
            x = x.astype(f32)
            xm_ref[b * PIX : (b + 1) * PIX, d * own : (d + 1) * own] = (x * sty).astype(bf16)
    products = jnp.dot(xm_ref[...], wslot_ref[...], preferred_element_type=f32)
    z = None
    for kx in range(3):
        total = None
        for ky in range(3):
            k = 3 * ky + kx
            moved = row_shift(products[:, k * own : (k + 1) * own], ky - 1)
            total = moved if total is None else total + moved
        total = col_shift(total, kx - 1)
        z = total if z is None else z + total
    z_ref[...] = z
    demod = jnp.concatenate(
        [jnp.broadcast_to(demod_ref[b : b + 1, :], (PIX, own)) for b in range(count)], axis=0
    )
    pre = demod * z + nb_ref[...]
    soft, sig = act_parts(pre)
    y = (root_two * (0.2 * pre + 0.8 * soft)).astype(bf16)
    slope_ref[...] = root_two * (0.2 + 0.8 * sig)
    rgb = rgb_ref[...]
    pay_ref[:pixels, :] = y
    pay_ref[pixels:, :] = rgb
    if second:
        refs[13][...] = lax.dot_general(rgb, y, NT, preferred_element_type=f32)[:8]


def first_image_kernel(*refs):
    out_ref = refs[-1]
    pixels = out_ref.shape[1]
    parts = [
        lax.dot_general(ref[pixels:, :], ref[:pixels, :], NT, preferred_element_type=f32)[:8]
        for ref in refs[:4]
    ]
    out_ref[...] = (parts[0] + parts[1]) + (parts[2] + parts[3])


def head_grad(dimage, rgb_ref):
    own = rgb_ref.shape[1]
    hi = dimage.astype(bf16).astype(f32)
    lo = dimage - hi
    left = pad_rows(jnp.concatenate([hi, lo], axis=0), own).T.astype(bf16)
    rgb = rgb_ref[...].astype(f32)[:8]
    right = jnp.concatenate([rgb, rgb], axis=0)
    return jnp.dot(left, pad_rows(right, own).astype(bf16), preferred_element_type=f32)


def store_gz(da, z, demod_ref, pay_ref):
    count, own = demod_ref.shape
    rows = []
    for b in range(count):
        demod = demod_ref[b : b + 1, :]
        part = da[b * PIX : (b + 1) * PIX]
        pay_ref[b * PIX : (b + 1) * PIX, :] = (part * demod).astype(bf16)
        d_demod = jnp.sum(part * z[b * PIX : (b + 1) * PIX], axis=0, keepdims=True)
        rows.append(-d_demod * demod * demod * demod)
    coef = jnp.concatenate(rows + [jnp.zeros((8 - count, own), f32)], axis=0)
    hi = coef.astype(bf16).astype(f32)
    pay_ref[count * PIX :, :] = jnp.concatenate([hi, coef - hi], axis=0).astype(bf16)


def shifted_gz(gz):
    gz = gz.astype(f32)
    by_col = [col_shift(gz, 1 - kx).astype(bf16) for kx in range(3)]
    return jnp.concatenate([row_shift(by_col[k % 3], 1 - k // 3) for k in range(TAPS)], axis=1)


def store_dx(cols, wslot_ref, stys_ref, keep_ref, send_ref):
    count = stys_ref.shape[0]
    own = keep_ref.shape[1]
    share = lax.dot_general(cols, wslot_ref[...], NT, preferred_element_type=f32)
    for d in range(4):
        for b in range(count):
            sty = stys_ref[b : b + 1, d * own : (d + 1) * own]
            block = share[b * PIX : (b + 1) * PIX, d * own : (d + 1) * own] * sty
            at = (d // 2) * count * PIX + b * PIX
            if d % 2 == 0:
                keep_ref[at : at + PIX, :] = block
            else:
                send_ref[at : at + PIX, :] = block.astype(bf16)


def disc_kernel(
    own_ref, r1_ref, r2_ref, r3_ref, first_ref, disc_ref, rgb_ref, slope_ref, z_ref, demod_ref,
    wslot_ref, stys_ref, tail_ref, pay_ref, keep_ref, send_ref,
):
    image = ((own_ref[...] + r1_ref[...]) + (r2_ref[...] + r3_ref[...])) + first_ref[...]
    lanes = 128
    per = PIX // lanes
    count = stys_ref.shape[0]
    out_rows, logits = [], []
    for b in range(count):
        logit = jnp.zeros((1, 1), f32)
        chunks = []
        for n in range(per):
            at = b * PIX + n * lanes
            q = disc_ref[3]
            for ch in range(3):
                q = q + disc_ref[ch] * image[ch : ch + 1, at : at + lanes]
            soft, sig = act_parts(q)
            hidden = 0.2 * q + 0.8 * soft
            logit = logit + jnp.sum(disc_ref[4] * hidden, keepdims=True)
            dq = (disc_ref[4] / PIX) * (0.2 + 0.8 * sig)
            chunks.append(
                [jnp.sum(disc_ref[ch] * dq, axis=0, keepdims=True) for ch in range(3)]
            )
        logit = logit / PIX
        e = jnp.exp(-jnp.abs(logit))
        g = -jnp.where(logit >= 0.0, e, 1.0) / (1.0 + e)
        rows = [jnp.concatenate([c[ch] for c in chunks], axis=1) * g for ch in range(3)]
        out_rows.append(jnp.concatenate(rows + [jnp.zeros((5, PIX), f32)], axis=0))
        wide = jnp.broadcast_to(logit, (1, lanes))
        hi = wide.astype(bf16).astype(f32)
        mid = (wide - hi).astype(bf16).astype(f32)
        logits += [hi, mid, wide - hi - mid]
    dimage = jnp.concatenate(out_rows, axis=1)
    pieces = [
        dimage[ch : ch + 1, n * lanes : (n + 1) * lanes] for ch in range(3) for n in range(count * per)
    ]
    high = jnp.concatenate(pieces, axis=0)
    low = high - high.astype(bf16).astype(f32)
    spare = TAIL - 2 * len(pieces) - len(logits)
    tail_ref[...] = jnp.concatenate(
        [high, low] + logits + [jnp.zeros((spare, lanes), f32)], axis=0
    ).astype(bf16)
    da = head_grad(dimage, rgb_ref) * slope_ref[...]
    store_gz(da, z_ref[...], demod_ref, pay_ref)
    cols = shifted_gz(pay_ref[: count * PIX, :])
    store_dx(cols, wslot_ref, stys_ref, keep_ref, send_ref)


def pair_kernel(keep_ref, got_ref, tail_ref, near_ref, far_ref):
    rows = far_ref.shape[0]
    near_ref[rows:, :] = tail_ref[...]
    near_ref[:rows, :] = (keep_ref[:rows] + got_ref[:rows].astype(f32)).astype(bf16)
    far_ref[...] = (keep_ref[rows:] + got_ref[rows:].astype(f32)).astype(bf16)


def first_grad_kernel(
    idx, s0_ref, s1_ref, rgb_ref, slope_ref, z_ref, demod_ref, other_ref, tail_ref,
    pay_ref, logit_ref,
):
    count = demod_ref.shape[0]
    pixels = count * PIX
    chunks = pixels // 128

    def put_logits(tail):
        for b in range(count):
            at = 6 * chunks + 3 * b
            logit_ref[b] = jnp.max((tail[at : at + 1] + tail[at + 1 : at + 2]) + tail[at + 2 : at + 3])

    @pl.when(idx[0] == 0)
    def _():
        dx = (s0_ref[:pixels, :].astype(f32) + s1_ref[...].astype(f32)).astype(bf16)
        tail = s0_ref[pixels:, :].astype(f32)
        put_logits(tail)
        both = tail[: 3 * chunks] + tail[3 * chunks : 6 * chunks]
        rows = [
            jnp.concatenate(
                [both[ch * chunks + n : ch * chunks + n + 1] for n in range(chunks)], axis=1
            )
            for ch in range(3)
        ]
        dimage = jnp.concatenate(rows + [jnp.zeros((5, pixels), f32)], axis=0)
        da = (head_grad(dimage, rgb_ref) + dx.astype(f32)) * slope_ref[...]
        store_gz(da, z_ref[...], demod_ref, pay_ref)

    @pl.when(idx[0] != 0)
    def _():
        put_logits(tail_ref[...].astype(f32))
        pay_ref[...] = other_ref[...]


def share_kernel(pay_ref, wslot_ref, stys_ref, xm_ref, keep_ref, send_ref, acc_ref):
    cols = shifted_gz(pay_ref[: stys_ref.shape[0] * PIX, :])
    store_dx(cols, wslot_ref, stys_ref, keep_ref, send_ref)
    acc_ref[...] = jnp.dot(xm_ref[: acc_ref.shape[0], :], cols, preferred_element_type=f32)


def dx_pair_kernel(keep_ref, got_ref, near_ref, far_ref):
    rows = near_ref.shape[0]
    near_ref[...] = keep_ref[:rows] + got_ref[:rows].astype(f32)
    far_ref[...] = (keep_ref[rows:] + got_ref[rows:].astype(f32)).astype(bf16)


def turn_kernel(idx, xa_ref, xb_ref, sty_ref, out_ref):
    chan = idx[1]
    full = xa_ref.shape[1]
    count = sty_ref.shape[0]
    own = full // 4

    def turn(ref):
        for d in range(4):
            start = pl.multiple_of((chan ^ d) * own, own)
            out_ref[pl.ds(start, own), :] = ref[:, d * own : (d + 1) * own].T

    @pl.when(idx[0] == 0)
    def _():
        turn(xa_ref)

    @pl.when(idx[0] != 0)
    def _():
        turn(xb_ref)

    sty = sty_ref[...]
    hi = sty.astype(bf16).astype(f32)
    mid = (sty - hi).astype(bf16).astype(f32)
    lo = sty - hi - mid
    rows = [hi, mid, lo]
    out_ref[full:, :] = jnp.concatenate(
        rows + [jnp.zeros((EXTRA - 3 * count, full), f32)], axis=0
    ).astype(bf16)


def z_partner(z, core):
    return ((z + core) ^ 1) - core


def weight_kernel(
    idx, pay_ref, other_pay_ref, xm_ref, other_xm_ref, w_ref, before_ref,
    keep_ref, send_1_ref, send_2_ref, send_3_ref, sum_ref,
):
    core, y, z = idx[1] & 1, idx[2], idx[3]
    full = before_ref.shape[0]
    own = pay_ref.shape[1]
    pixels = pay_ref.shape[0] - EXTRA
    count = pixels // PIX
    cols = shifted_gz(other_pay_ref[:pixels, :])
    total = before_ref[...] + jnp.dot(other_xm_ref[:full, :], cols, preferred_element_type=f32)
    sty_rows, coef_rows = [], []
    for pay, xm in ((pay_ref, xm_ref), (other_pay_ref, other_xm_ref)):
        tail = xm[full:, :].astype(f32)
        sty = tail[:count] + tail[count : 2 * count] + tail[2 * count : 3 * count]
        sty_rows.append(sty * sty)
        tail = pay[pixels:, :].astype(f32)
        coef_rows.append(tail[:count] + tail[8 : 8 + count])
    left = pad_rows(jnp.concatenate(sty_rows, axis=0), own).T
    right = pad_rows(jnp.concatenate(coef_rows, axis=0), own)
    demod_term = jnp.dot(left, right, precision=lax.Precision.HIGHEST, preferred_element_type=f32)
    for k in range(TAPS):
        at = slice(k * full, (k + 1) * full)
        sum_ref[at, :] = total[:, k * own : (k + 1) * own] + w_ref[at, :].astype(f32) * demod_term
    rows = keep_ref.shape[0] // 4
    step = 1 - 2 * core
    for d, ref in enumerate((keep_ref, send_1_ref, send_2_ref, send_3_ref)):
        to_y = (y + step * d) & 3
        for e in range(4):
            start = (to_y * 8 + ((z + 2 * e) & 7)) * rows
            block = sum_ref[pl.ds(pl.multiple_of(start, RES), rows), :]
            ref[e * rows : (e + 1) * rows, :] = block.astype(ref.dtype)


def y_sum_kernel(keep_ref, r1_ref, r2_ref, r3_ref, own_ref, *out_refs):
    rows = own_ref.shape[0]
    for e, ref in enumerate((own_ref, *out_refs)):
        at = slice(e * rows, (e + 1) * rows)
        total = keep_ref[at] + r1_ref[at].astype(f32)
        total = total + (r2_ref[at].astype(f32) + r3_ref[at].astype(f32))
        ref[...] = total.astype(ref.dtype)


def total_kernel(count, *refs):
    grad_ref, dx_ref = refs[-2:]
    total = refs[0][...].astype(f32)
    for ref in refs[1:count]:
        total = total + ref[...].astype(f32)
    grad_ref[...] = total
    dx = (refs[count][...] + refs[count + 1][...].astype(f32)).astype(bf16)
    for b in range(dx_ref.shape[0]):
        dx_ref[b] = dx[b * PIX : (b + 1) * PIX].T


def call(kernel, outs, args, scratch=(), scalars=0, raws=0, keep=True):
    smem = pl.BlockSpec(memory_space=pltpu.SMEM)
    vmem = pl.BlockSpec(memory_space=pltpu.VMEM)
    plain = scalars + raws
    args = (
        list(args[:scalars])
        + [pltpu.with_memory_space_constraint(a, pltpu.HBM) for a in args[scalars:plain]]
        + [pltpu.with_memory_space_constraint(a, pltpu.VMEM) for a in args[plain:]]
    )
    hbm = pl.BlockSpec(memory_space=pltpu.HBM)
    place = pltpu.VMEM if keep else jax.ShapeDtypeStruct
    return pl.pallas_call(
        kernel,
        out_shape=[
            jax.ShapeDtypeStruct(*o[:2]) if len(o) > 2 else place(*o) for o in outs
        ],
        in_specs=[smem] * scalars + [hbm] * raws + [vmem] * (len(args) - plain),
        out_specs=[smem if len(o) > 2 else vmem for o in outs],
        scratch_shapes=list(scratch),
        compiler_params=pltpu.CompilerParams(vmem_limit_bytes=20 * 2**20),
    )(*args)


def body(
    base, style, noise, conv_weight, conv_bias, noise_gain, rgb_weight, disc_weight, disc_bias,
    disc_out,
):
    weight, styles, noises, rgb = conv_weight[0], style[0], noise[0], rgb_weight[0]
    own = weight.shape[1]
    full = weight.shape[0] // TAPS
    count = base.shape[0]
    pixels = count * PIX
    dp_index = lax.axis_index("dp")
    idx = jnp.stack(
        [lax.axis_index("segment"), lax.axis_index("chan"), dp_index // 8, dp_index % 8]
    ).astype(jnp.int32)

    def across(value, links):
        return lax.ppermute(value, ("segment", "chan"), links)

    def by_core(value, place):
        links = []
        for y in range(4):
            for z in range(8):
                for c in range(4):
                    to_y, to_z = place(y, z, c % 2)
                    links.append(((y * 8 + z) * 4 + c, (to_y % 4 * 8 + to_z % 8) * 4 + c))
        return lax.ppermute(value, ("dp", "chan"), links)

    def over_y(value, d):
        return by_core(value, lambda y, z, core: (y - d if core else y + d, z))

    def over_z(value, d):
        return lax.ppermute(
            value, "dp", [(y * 8 + z, y * 8 + (z + d) % 8) for y in range(4) for z in range(8)]
        )

    def flip(value, d):
        return across(value, [(s * 4 + c, (1 - s) * 4 + (c ^ d)) for s in range(2) for c in range(4)])

    def within(value, d):
        return across(value, [(s * 4 + c, s * 4 + (c ^ d)) for s in range(2) for c in range(4)])

    x2 = flip(base, 2)
    x1 = within(base, 1)
    x3 = within(x2, 1)
    sources = [
        weight, styles, noises, noise_gain, conv_bias, disc_weight, disc_bias[None], disc_out[None],
        rgb,
    ]
    wslot, stys, demod, nb, disc, rgbp, sty = call(
        prep_kernel,
        [
            ((full, TAPS * own), bf16),
            ((count, full), f32),
            ((count, own), f32),
            ((pixels, own), f32),
            ((5, disc_weight.shape[1], own), f32),
            ((EXTRA, own), bf16),
            ((count, full), f32),
        ],
        [idx, *sources],
        scratch=[pltpu.VMEM(a.shape, a.dtype) for a in sources]
        + [pltpu.SemaphoreType.DMA((len(sources),))],
        scalars=1,
        raws=len(sources),
    )
    conv_outs = [
        ((pixels + EXTRA, own), bf16),
        ((pixels, own), f32),
        ((pixels, own), f32),
        ((pixels, full), bf16),
    ]
    pay, slope_a, z_a, xm_a = call(
        functools.partial(conv_kernel, False),
        conv_outs,
        [base, x1, x2, x3, stys, wslot, demod, nb, rgbp],
    )
    y0 = flip(pay, 0)
    y2 = flip(pay, 2)
    y1 = within(y0, 1)
    y3 = within(y2, 1)
    _, slope_b, z_b, xm_b, image_own = call(
        functools.partial(conv_kernel, True),
        conv_outs + [((8, pixels), f32)],
        [y0, y1, y2, y3, stys, wslot, demod, nb, rgbp],
    )
    images = [within(image_own, d) for d in (1, 2, 3)]
    (xm,) = call(turn_kernel, [((full + EXTRA, pixels), bf16)], [idx, xm_a, xm_b, sty], scalars=1)
    (image_first,) = call(first_image_kernel, [((8, pixels), f32)], [y0, y1, y2, y3])

    def to_partner(value):
        return by_core(value, lambda y, z, core: (y, z_partner(z, core)))

    other_xm = to_partner(xm)
    two = (2 * pixels, own)
    tail, pay_b, dx_keep, dx_send = call(
        disc_kernel,
        [((TAIL, own), bf16), ((pixels + EXTRA, own), bf16), (two, f32), (two, bf16)],
        [image_own, *images, image_first, disc, rgbp, slope_b, z_b, demod, wslot, stys],
    )
    dx_got = within(dx_send, 1)
    share = ((pixels, own), bf16)
    dx_near, dx_far = call(
        pair_kernel, [((pixels + TAIL, own), bf16), share], [dx_keep, dx_got, tail]
    )
    got = [flip(dx_near, 0), flip(dx_far, 2)]
    pay_g, logits = call(
        first_grad_kernel,
        [((pixels + EXTRA, own), bf16), ((count,), f32, True)],
        [idx, *got, rgbp, slope_a, z_a, demod, pay_b, tail],
        scalars=1,
    )
    other_pay = to_partner(pay_g)
    keep, send, before = call(
        share_kernel, [(two, f32), (two, bf16), ((full, TAPS * own), f32)], [pay_g, wslot, stys, xm]
    )
    got = within(send, 1)
    near, far = call(dx_pair_kernel, [((pixels, own), f32), share], [keep, got])
    mine = [near, within(far, 2)]
    rows = weight.shape[0] // 32
    four = (4 * rows, own)
    y_keep, *y_send = call(
        weight_kernel,
        [(four, f32)] + [(four, bf16)] * 3,
        [idx, pay_g, other_pay, xm, other_xm, weight, before],
        scratch=[pltpu.VMEM(weight.shape, f32)],
        scalars=1,
    )
    y_got = [over_y(y_send[d - 1], d) for d in (1, 2, 3)]
    block = (rows, own)
    z_own, *z_outs = call(y_sum_kernel, [(block, f32)] + [(block, bf16)] * 3, [y_keep, *y_got])
    parts = [z_own] + [over_z(z_outs[e - 1], 2 * e) for e in (1, 2, 3)]
    grad_rows, dx = call(
        functools.partial(total_kernel, len(parts)),
        [((rows, own), f32), ((count, own, PIX), bf16)],
        [*parts, *mine],
        keep=False,
    )
    return (grad_rows[None], logits, dx[None])


def solution(mesh):
    placed = (
        P("dp", "chan", None),
        P("segment", "dp", None),
        P("segment", "dp", None),
        P("segment", None, "chan"),
        P("segment", "chan"),
        P("segment", "chan"),
        P("segment", None, "chan"),
        P(),
        P(),
        P(),
    )
    return jax.shard_map(
        body,
        mesh=mesh,
        in_specs=placed,
        out_specs=(P("segment", "dp", "chan"), P("dp"), P("segment", "dp", "chan", None)),
        check_vma=False,
    )
```

```python
import functools

import jax
import jax.numpy as jnp
from jax import lax
from jax.experimental import pallas as pl
from jax.experimental.pallas import tpu as pltpu
from jax.sharding import PartitionSpec as P


RES = 16
PIX = RES * RES
TAPS = 9
EXTRA = 16
TAIL = 32
epsilon = 1e-06
root_two = 1.4142135623730951
f32 = jnp.float32
bf16 = jnp.bfloat16


NT = (((1,), (1,)), ((), ()))


def act_parts(t):
    e = jnp.exp(-jnp.abs(t))
    r = 1.0 / (1.0 + e)
    soft = jnp.maximum(t, 0.0) + jnp.log(1.0 + e)
    sig = jnp.where(t >= 0.0, r, e * r)
    return soft, sig


def row_shift(v, a):
    if a == 0:
        return v
    zeros = jnp.zeros((RES, v.shape[1]), v.dtype)
    parts = []
    for b in range(v.shape[0] // PIX):
        base = b * PIX
        if a > 0:
            parts += [v[base + RES : base + PIX], zeros]
        else:
            parts += [zeros, v[base : base + PIX - RES]]
    return jnp.concatenate(parts, axis=0)


def col_shift(v, b):
    if b == 0:
        return v
    x = lax.broadcasted_iota(jnp.int32, v.shape, 0) & (RES - 1)
    if b > 0:
        return jnp.where(x < RES - 1, pltpu.roll(v, v.shape[0] - 1, 0), 0.0)
    return jnp.where(x > 0, pltpu.roll(v, 1, 0), 0.0)


def pad_rows(v, rows):
    return jnp.concatenate([v, jnp.zeros((rows - v.shape[0], v.shape[1]), v.dtype)], axis=0)


def prep_kernel(idx, *refs):
    number = (len(refs) - 8) // 2
    sources, outs, copies = refs[:number], refs[number : number + 7], refs[number + 7 : -1]
    sem = refs[-1]
    moves = [
        pltpu.make_async_copy(src, dst, sem.at[n]) for n, (src, dst) in enumerate(zip(sources, copies))
    ]
    for move in moves:
        move.start()
    for move in moves:
        move.wait()
    w_ref, sty_ref, noise_ref, gain_ref, bias_ref, dw_ref, db_ref, do_ref, rgb_ref = copies
    wslot_ref, stys_ref, demod_ref, nb_ref, disc_ref, rgbp_ref, stycopy_ref = outs
    rgbp_ref[...] = pad_rows(rgb_ref[...], EXTRA)
    stycopy_ref[...] = sty_ref[...]
    chan = idx[1]
    own = w_ref.shape[1]
    full = w_ref.shape[0] // TAPS
    count = sty_ref.shape[0]
    chans = full // own
    for d in range(chans):
        part = chan ^ d
        for k in range(TAPS):
            start = pl.multiple_of(k * full + part * own, own)
            wslot_ref[d * own : (d + 1) * own, k * own : (k + 1) * own] = w_ref[pl.ds(start, own), :]
        stys_ref[:, d * own : (d + 1) * own] = sty_ref[:, pl.ds(pl.multiple_of(part * own, own), own)]
    squares = jnp.zeros((full, own), f32)
    for k in range(TAPS):
        w = w_ref[k * full : (k + 1) * full, :].astype(f32)
        squares = squares + w * w
    sty = sty_ref[...]
    cols = pad_rows(sty * sty, own).T
    for b in range(count):
        total = jnp.sum(cols[:, b : b + 1] * squares, axis=0, keepdims=True)
        demod_ref[b : b + 1, :] = lax.rsqrt(total + epsilon)
        noise = jnp.broadcast_to(noise_ref[b : b + 1, :], (own, PIX)).T
        nb_ref[b * PIX : (b + 1) * PIX, :] = gain_ref[...] * noise + bias_ref[...]
    rows = [dw_ref[0:1, :], dw_ref[1:2, :], dw_ref[2:3, :], db_ref[...], do_ref[...]]
    for n, row in enumerate(rows):
        disc_ref[n] = jnp.broadcast_to(row, (own, row.shape[1])).T


def conv_kernel(second, *refs):
    x_refs = refs[:4]
    stys_ref, wslot_ref, demod_ref, nb_ref, rgb_ref = refs[4:9]
    pay_ref, slope_ref, z_ref, xm_ref = refs[9:13]
    count = stys_ref.shape[0]
    own = demod_ref.shape[1]
    pixels = count * PIX
    for d in range(4):
        for b in range(count):
            sty = stys_ref[b : b + 1, d * own : (d + 1) * own]
            x = x_refs[d][b * PIX : (b + 1) * PIX, :] if second else x_refs[d][b].T
            x = x.astype(f32)
            xm_ref[b * PIX : (b + 1) * PIX, d * own : (d + 1) * own] = (x * sty).astype(bf16)
    products = jnp.dot(xm_ref[...], wslot_ref[...], preferred_element_type=f32)
    z = None
    for kx in range(3):
        total = None
        for ky in range(3):
            k = 3 * ky + kx
            moved = row_shift(products[:, k * own : (k + 1) * own], ky - 1)
            total = moved if total is None else total + moved
        total = col_shift(total, kx - 1)
        z = total if z is None else z + total
    z_ref[...] = z
    demod = jnp.concatenate(
        [jnp.broadcast_to(demod_ref[b : b + 1, :], (PIX, own)) for b in range(count)], axis=0
    )
    pre = demod * z + nb_ref[...]
    soft, sig = act_parts(pre)
    y = (root_two * (0.2 * pre + 0.8 * soft)).astype(bf16)
    slope_ref[...] = root_two * (0.2 + 0.8 * sig)
    rgb = rgb_ref[...]
    pay_ref[:pixels, :] = y
    pay_ref[pixels:, :] = rgb
    if second:
        refs[13][...] = lax.dot_general(rgb, y, NT, preferred_element_type=f32)[:8]


def image_pair_kernel(own_ref, got_ref, out_ref):
    out_ref[...] = own_ref[...] + got_ref[...]


def first_image_kernel(*refs):
    out_ref = refs[-1]
    pixels = out_ref.shape[1]
    parts = [
        lax.dot_general(ref[pixels:, :], ref[:pixels, :], NT, preferred_element_type=f32)[:8]
        for ref in refs[:4]
    ]
    out_ref[...] = (parts[0] + parts[1]) + (parts[2] + parts[3])


def head_grad(dimage, rgb_ref):
    own = rgb_ref.shape[1]
    hi = dimage.astype(bf16).astype(f32)
    lo = dimage - hi
    left = pad_rows(jnp.concatenate([hi, lo], axis=0), own).T.astype(bf16)
    rgb = rgb_ref[...].astype(f32)[:8]
    right = jnp.concatenate([rgb, rgb], axis=0)
    return jnp.dot(left, pad_rows(right, own).astype(bf16), preferred_element_type=f32)


def store_gz(da, z, demod_ref, pay_ref):
    count, own = demod_ref.shape
    rows = []
    for b in range(count):
        demod = demod_ref[b : b + 1, :]
        part = da[b * PIX : (b + 1) * PIX]
        pay_ref[b * PIX : (b + 1) * PIX, :] = (part * demod).astype(bf16)
        d_demod = jnp.sum(part * z[b * PIX : (b + 1) * PIX], axis=0, keepdims=True)
        rows.append(-d_demod * demod * demod * demod)
    coef = jnp.concatenate(rows + [jnp.zeros((8 - count, own), f32)], axis=0)
    hi = coef.astype(bf16).astype(f32)
    pay_ref[count * PIX :, :] = jnp.concatenate([hi, coef - hi], axis=0).astype(bf16)


def shifted_gz(gz):
    gz = gz.astype(f32)
    by_col = [col_shift(gz, 1 - kx).astype(bf16) for kx in range(3)]
    return jnp.concatenate([row_shift(by_col[k % 3], 1 - k // 3) for k in range(TAPS)], axis=1)


def store_dx(cols, wslot_ref, stys_ref, keep_ref, send_ref):
    count = stys_ref.shape[0]
    own = keep_ref.shape[1]
    share = lax.dot_general(cols, wslot_ref[...], NT, preferred_element_type=f32)
    for d in range(4):
        for b in range(count):
            sty = stys_ref[b : b + 1, d * own : (d + 1) * own]
            block = share[b * PIX : (b + 1) * PIX, d * own : (d + 1) * own] * sty
            at = (d // 2) * count * PIX + b * PIX
            if d % 2 == 0:
                keep_ref[at : at + PIX, :] = block
            else:
                send_ref[at : at + PIX, :] = block.astype(bf16)


def disc_kernel(
    own_ref, other_ref, first_ref, disc_ref, rgb_ref, slope_ref, z_ref, demod_ref,
    wslot_ref, stys_ref, tail_ref, pay_ref, keep_ref, send_ref,
):
    image = (own_ref[...] + other_ref[...]) + first_ref[...]
    lanes = 128
    per = PIX // lanes
    count = stys_ref.shape[0]
    out_rows, logits = [], []
    for b in range(count):
        logit = jnp.zeros((1, 1), f32)
        chunks = []
        for n in range(per):
            at = b * PIX + n * lanes
            q = disc_ref[3]
            for ch in range(3):
                q = q + disc_ref[ch] * image[ch : ch + 1, at : at + lanes]
            soft, sig = act_parts(q)
            hidden = 0.2 * q + 0.8 * soft
            logit = logit + jnp.sum(disc_ref[4] * hidden, keepdims=True)
            dq = (disc_ref[4] / PIX) * (0.2 + 0.8 * sig)
            chunks.append(
                [jnp.sum(disc_ref[ch] * dq, axis=0, keepdims=True) for ch in range(3)]
            )
        logit = logit / PIX
        e = jnp.exp(-jnp.abs(logit))
        under = 1.0 + e
        g = jnp.where(logit >= 0.0, (1.0 - under) / under, e / under - 1.0)
        rows = [jnp.concatenate([c[ch] for c in chunks], axis=1) * g for ch in range(3)]
        out_rows.append(jnp.concatenate(rows + [jnp.zeros((5, PIX), f32)], axis=0))
        wide = jnp.broadcast_to(logit, (1, lanes))
        hi = wide.astype(bf16).astype(f32)
        mid = (wide - hi).astype(bf16).astype(f32)
        logits += [hi, mid, wide - hi - mid]
    dimage = jnp.concatenate(out_rows, axis=1)
    pieces = [
        dimage[ch : ch + 1, n * lanes : (n + 1) * lanes] for ch in range(3) for n in range(count * per)
    ]
    high = jnp.concatenate(pieces, axis=0)
    low = high - high.astype(bf16).astype(f32)
    spare = TAIL - 2 * len(pieces) - len(logits)
    tail_ref[...] = jnp.concatenate(
        [high, low] + logits + [jnp.zeros((spare, lanes), f32)], axis=0
    ).astype(bf16)
    da = head_grad(dimage, rgb_ref) * slope_ref[...]
    store_gz(da, z_ref[...], demod_ref, pay_ref)
    cols = shifted_gz(pay_ref[: count * PIX, :])
    store_dx(cols, wslot_ref, stys_ref, keep_ref, send_ref)


def pair_kernel(keep_ref, got_ref, tail_ref, near_ref, far_ref):
    rows = far_ref.shape[0]
    near_ref[rows:, :] = tail_ref[...]
    near_ref[:rows, :] = (keep_ref[:rows] + got_ref[:rows].astype(f32)).astype(bf16)
    far_ref[...] = (keep_ref[rows:] + got_ref[rows:].astype(f32)).astype(bf16)


def first_grad_kernel(
    idx, s0_ref, s1_ref, rgb_ref, slope_ref, z_ref, demod_ref, other_ref, tail_ref,
    pay_ref, logit_ref,
):
    count = demod_ref.shape[0]
    pixels = count * PIX
    chunks = pixels // 128

    def put_logits(tail):
        for b in range(count):
            at = 6 * chunks + 3 * b
            logit_ref[b] = jnp.max((tail[at : at + 1] + tail[at + 1 : at + 2]) + tail[at + 2 : at + 3])

    @pl.when(idx[0] == 0)
    def _():
        dx = (s0_ref[:pixels, :].astype(f32) + s1_ref[...].astype(f32)).astype(bf16)
        tail = s0_ref[pixels:, :].astype(f32)
        put_logits(tail)
        both = tail[: 3 * chunks] + tail[3 * chunks : 6 * chunks]
        rows = [
            jnp.concatenate(
                [both[ch * chunks + n : ch * chunks + n + 1] for n in range(chunks)], axis=1
            )
            for ch in range(3)
        ]
        dimage = jnp.concatenate(rows + [jnp.zeros((5, pixels), f32)], axis=0)
        da = (head_grad(dimage, rgb_ref) + dx.astype(f32)) * slope_ref[...]
        store_gz(da, z_ref[...], demod_ref, pay_ref)

    @pl.when(idx[0] != 0)
    def _():
        put_logits(tail_ref[...].astype(f32))
        pay_ref[...] = other_ref[...]


def share_kernel(pay_ref, wslot_ref, stys_ref, xm_ref, keep_ref, send_ref, acc_ref):
    cols = shifted_gz(pay_ref[: stys_ref.shape[0] * PIX, :])
    store_dx(cols, wslot_ref, stys_ref, keep_ref, send_ref)
    acc_ref[...] = jnp.dot(xm_ref[: acc_ref.shape[0], :], cols, preferred_element_type=f32)


def dx_pair_kernel(keep_ref, got_ref, near_ref, far_ref):
    rows = near_ref.shape[0]
    near_ref[...] = keep_ref[:rows] + got_ref[:rows].astype(f32)
    far_ref[...] = (keep_ref[rows:] + got_ref[rows:].astype(f32)).astype(bf16)


def turn_kernel(idx, xa_ref, xb_ref, sty_ref, out_ref):
    chan = idx[1]
    full = xa_ref.shape[1]
    count = sty_ref.shape[0]
    own = full // 4

    def turn(ref):
        for d in range(4):
            start = pl.multiple_of((chan ^ d) * own, own)
            out_ref[pl.ds(start, own), :] = ref[:, d * own : (d + 1) * own].T

    @pl.when(idx[0] == 0)
    def _():
        turn(xa_ref)

    @pl.when(idx[0] != 0)
    def _():
        turn(xb_ref)

    sty = sty_ref[...]
    hi = sty.astype(bf16).astype(f32)
    mid = (sty - hi).astype(bf16).astype(f32)
    lo = sty - hi - mid
    rows = [hi, mid, lo]
    out_ref[full:, :] = jnp.concatenate(
        rows + [jnp.zeros((EXTRA - 3 * count, full), f32)], axis=0
    ).astype(bf16)


def z_partner(z, core):
    return ((z + core) ^ 1) - core


def weight_kernel(
    idx, pay_ref, other_pay_ref, xm_ref, other_xm_ref, w_ref, before_ref,
    keep_ref, send_1_ref, send_2_ref, send_3_ref, sum_ref,
):
    core, y, z = idx[1] & 1, idx[2], idx[3]
    full = before_ref.shape[0]
    own = pay_ref.shape[1]
    pixels = pay_ref.shape[0] - EXTRA
    count = pixels // PIX
    cols = shifted_gz(other_pay_ref[:pixels, :])
    other_xm = other_xm_ref[:full, :]
    sty_rows, coef_rows = [], []
    for pay, xm in ((pay_ref, xm_ref), (other_pay_ref, other_xm_ref)):
        tail = xm[full:, :].astype(f32)
        sty = tail[:count] + tail[count : 2 * count] + tail[2 * count : 3 * count]
        sty_rows.append(sty * sty)
        tail = pay[pixels:, :].astype(f32)
        coef_rows.append(tail[:count] + tail[8 : 8 + count])
    left = pad_rows(jnp.concatenate(sty_rows, axis=0), own).T
    right = pad_rows(jnp.concatenate(coef_rows, axis=0), own)
    demod_term = jnp.dot(left, right, precision=lax.Precision.HIGHEST, preferred_element_type=f32)
    for first in range(0, TAPS, 2):
        taps = range(first, min(first + 2, TAPS))
        lanes = slice(first * own, (taps[-1] + 1) * own)
        total = before_ref[:, lanes] + jnp.dot(
            other_xm, cols[:, lanes], preferred_element_type=f32
        )
        for n, k in enumerate(taps):
            at = slice(k * full, (k + 1) * full)
            w = w_ref[at, :].astype(f32)
            sum_ref[at, :] = total[:, n * own : (n + 1) * own] + w * demod_term
    rows = keep_ref.shape[0] // 4
    step = 1 - 2 * core
    for d, ref in enumerate((keep_ref, send_1_ref, send_2_ref, send_3_ref)):
        to_y = (y + step * d) & 3
        for e in range(4):
            start = (to_y * 8 + ((z + 2 * e) & 7)) * rows
            block = sum_ref[pl.ds(pl.multiple_of(start, RES), rows), :]
            ref[e * rows : (e + 1) * rows, :] = block.astype(ref.dtype)


def y_sum_kernel(keep_ref, r1_ref, r2_ref, r3_ref, own_ref, *out_refs):
    rows = own_ref.shape[0]
    for e, ref in enumerate((own_ref, *out_refs)):
        at = slice(e * rows, (e + 1) * rows)
        total = keep_ref[at] + r1_ref[at].astype(f32)
        total = total + (r2_ref[at].astype(f32) + r3_ref[at].astype(f32))
        ref[...] = total.astype(ref.dtype)


def total_kernel(*refs):
    total = refs[0][...].astype(f32)
    for ref in refs[1:-1]:
        total = total + ref[...].astype(f32)
    refs[-1][...] = total


def input_grad_kernel(near_ref, far_ref, dx_ref):
    dx = (near_ref[...] + far_ref[...].astype(f32)).astype(bf16)
    for b in range(dx_ref.shape[0]):
        dx_ref[b] = dx[b * PIX : (b + 1) * PIX].T


def call(kernel, outs, args, scratch=(), scalars=0, raws=0, keep=True):
    smem = pl.BlockSpec(memory_space=pltpu.SMEM)
    vmem = pl.BlockSpec(memory_space=pltpu.VMEM)
    plain = scalars + raws
    args = (
        list(args[:scalars])
        + [pltpu.with_memory_space_constraint(a, pltpu.HBM) for a in args[scalars:plain]]
        + [pltpu.with_memory_space_constraint(a, pltpu.VMEM) for a in args[plain:]]
    )
    hbm = pl.BlockSpec(memory_space=pltpu.HBM)
    place = pltpu.VMEM if keep else jax.ShapeDtypeStruct
    return pl.pallas_call(
        kernel,
        out_shape=[
            jax.ShapeDtypeStruct(*o[:2]) if len(o) > 2 else place(*o) for o in outs
        ],
        in_specs=[smem] * scalars + [hbm] * raws + [vmem] * (len(args) - plain),
        out_specs=[smem if len(o) > 2 else vmem for o in outs],
        scratch_shapes=list(scratch),
        compiler_params=pltpu.CompilerParams(vmem_limit_bytes=20 * 2**20),
    )(*args)


def body(
    base, style, noise, conv_weight, conv_bias, noise_gain, rgb_weight, disc_weight, disc_bias,
    disc_out,
):
    weight, styles, noises, rgb = conv_weight[0], style[0], noise[0], rgb_weight[0]
    own = weight.shape[1]
    full = weight.shape[0] // TAPS
    count = base.shape[0]
    pixels = count * PIX
    dp_index = lax.axis_index("dp")
    idx = jnp.stack(
        [lax.axis_index("segment"), lax.axis_index("chan"), dp_index // 8, dp_index % 8]
    ).astype(jnp.int32)

    def across(value, links):
        return lax.ppermute(value, ("segment", "chan"), links)

    def by_core(value, place):
        links = []
        for y in range(4):
            for z in range(8):
                for c in range(4):
                    to_y, to_z = place(y, z, c % 2)
                    links.append(((y * 8 + z) * 4 + c, (to_y % 4 * 8 + to_z % 8) * 4 + c))
        return lax.ppermute(value, ("dp", "chan"), links)

    def over_y(value, d):
        return by_core(value, lambda y, z, core: (y - d if core else y + d, z))

    def over_z(value, d):
        return lax.ppermute(
            value, "dp", [(y * 8 + z, y * 8 + (z + d) % 8) for y in range(4) for z in range(8)]
        )

    def flip(value, d):
        return across(value, [(s * 4 + c, (1 - s) * 4 + (c ^ d)) for s in range(2) for c in range(4)])

    def within(value, d):
        return across(value, [(s * 4 + c, s * 4 + (c ^ d)) for s in range(2) for c in range(4)])

    x2 = flip(base, 2)
    x1 = within(base, 1)
    x3 = within(x2, 1)
    sources = [
        weight, styles, noises, noise_gain, conv_bias, disc_weight, disc_bias[None], disc_out[None],
        rgb,
    ]
    wslot, stys, demod, nb, disc, rgbp, sty = call(
        prep_kernel,
        [
            ((full, TAPS * own), bf16),
            ((count, full), f32),
            ((count, own), f32),
            ((pixels, own), f32),
            ((5, disc_weight.shape[1], own), f32),
            ((EXTRA, own), bf16),
            ((count, full), f32),
        ],
        [idx, *sources],
        scratch=[pltpu.VMEM(a.shape, a.dtype) for a in sources]
        + [pltpu.SemaphoreType.DMA((len(sources),))],
        scalars=1,
        raws=len(sources),
    )
    conv_outs = [
        ((pixels + EXTRA, own), bf16),
        ((pixels, own), f32),
        ((pixels, own), f32),
        ((pixels, full), bf16),
    ]
    pay, slope_a, z_a, xm_a = call(
        functools.partial(conv_kernel, False),
        conv_outs,
        [base, x1, x2, x3, stys, wslot, demod, nb, rgbp],
    )
    y0 = flip(pay, 0)
    y2 = flip(pay, 2)
    y1 = within(y0, 1)
    y3 = within(y2, 1)
    _, slope_b, z_b, xm_b, image_own = call(
        functools.partial(conv_kernel, True),
        conv_outs + [((8, pixels), f32)],
        [y0, y1, y2, y3, stys, wslot, demod, nb, rgbp],
    )
    image_got = within(image_own, 1)
    (image_chip,) = call(image_pair_kernel, [((8, pixels), f32)], [image_own, image_got])
    image_other = within(image_chip, 2)
    (xm,) = call(turn_kernel, [((full + EXTRA, pixels), bf16)], [idx, xm_a, xm_b, sty], scalars=1)
    (image_first,) = call(first_image_kernel, [((8, pixels), f32)], [y0, y1, y2, y3])

    def to_partner(value):
        return by_core(value, lambda y, z, core: (y, z_partner(z, core)))

    other_xm = to_partner(xm)
    two = (2 * pixels, own)
    tail, pay_b, dx_keep, dx_send = call(
        disc_kernel,
        [((TAIL, own), bf16), ((pixels + EXTRA, own), bf16), (two, f32), (two, bf16)],
        [image_chip, image_other, image_first, disc, rgbp, slope_b, z_b, demod, wslot, stys],
    )
    dx_got = within(dx_send, 1)
    share = ((pixels, own), bf16)
    dx_near, dx_far = call(
        pair_kernel, [((pixels + TAIL, own), bf16), share], [dx_keep, dx_got, tail]
    )
    got = [flip(dx_near, 0), flip(dx_far, 2)]
    pay_g, logits = call(
        first_grad_kernel,
        [((pixels + EXTRA, own), bf16), ((count,), f32, True)],
        [idx, *got, rgbp, slope_a, z_a, demod, pay_b, tail],
        scalars=1,
    )
    other_pay = to_partner(pay_g)
    keep, send, before = call(
        share_kernel, [(two, f32), (two, bf16), ((full, TAPS * own), f32)], [pay_g, wslot, stys, xm]
    )
    got = within(send, 1)
    near, far = call(dx_pair_kernel, [((pixels, own), f32), share], [keep, got])
    mine = [near, within(far, 2)]
    rows = weight.shape[0] // 32
    four = (4 * rows, own)
    y_keep, *y_send = call(
        weight_kernel,
        [(four, f32)] + [(four, bf16)] * 3,
        [idx, pay_g, other_pay, xm, other_xm, weight, before],
        scratch=[pltpu.VMEM(weight.shape, f32)],
        scalars=1,
    )
    y_got = [over_y(y_send[d - 1], d) for d in (1, 2, 3)]
    block = (rows, own)
    z_own, *z_outs = call(y_sum_kernel, [(block, f32)] + [(block, bf16)] * 3, [y_keep, *y_got])
    parts = [z_own] + [over_z(z_outs[e - 1], 2 * e) for e in (1, 2, 3)]
    (dx,) = call(input_grad_kernel, [((count, own, PIX), bf16)], mine, keep=False)
    (grad_rows,) = call(total_kernel, [((rows, own), f32)], parts, keep=False)
    return (grad_rows[None], logits, dx[None])


def solution(mesh):
    placed = (
        P("dp", "chan", None),
        P("segment", "dp", None),
        P("segment", "dp", None),
        P("segment", None, "chan"),
        P("segment", "chan"),
        P("segment", "chan"),
        P("segment", None, "chan"),
        P(),
        P(),
        P(),
    )
    return jax.shard_map(
        body,
        mesh=mesh,
        in_specs=placed,
        out_specs=(P("segment", "dp", "chan"), P("dp"), P("segment", "dp", "chan", None)),
        check_vma=False,
    )
```

```python
import functools

import jax
import jax.numpy as jnp
from jax import lax
from jax.experimental import pallas as pl
from jax.experimental.pallas import tpu as pltpu
from jax.sharding import PartitionSpec as P


RES = 16
PIX = RES * RES
TAPS = 9
EXTRA = 16
TAIL = 32
epsilon = 1e-06
root_two = 1.4142135623730951
f32 = jnp.float32
bf16 = jnp.bfloat16


NT = (((1,), (1,)), ((), ()))


def act_parts(t):
    e = jnp.exp(-jnp.abs(t))
    r = 1.0 / (1.0 + e)
    soft = jnp.maximum(t, 0.0) + jnp.log(1.0 + e)
    sig = jnp.where(t >= 0.0, r, e * r)
    return soft, sig


def row_shift(v, a):
    if a == 0:
        return v
    zeros = jnp.zeros((RES, v.shape[1]), v.dtype)
    parts = []
    for b in range(v.shape[0] // PIX):
        base = b * PIX
        if a > 0:
            parts += [v[base + RES : base + PIX], zeros]
        else:
            parts += [zeros, v[base : base + PIX - RES]]
    return jnp.concatenate(parts, axis=0)


def col_shift(v, b):
    if b == 0:
        return v
    x = lax.broadcasted_iota(jnp.int32, v.shape, 0) & (RES - 1)
    if b > 0:
        return jnp.where(x < RES - 1, pltpu.roll(v, v.shape[0] - 1, 0), 0.0)
    return jnp.where(x > 0, pltpu.roll(v, 1, 0), 0.0)


def pad_rows(v, rows):
    return jnp.concatenate([v, jnp.zeros((rows - v.shape[0], v.shape[1]), v.dtype)], axis=0)


def prep_kernel(idx, *refs):
    number = (len(refs) - 8) // 2
    sources, outs, copies = refs[:number], refs[number : number + 7], refs[number + 7 : -1]
    sem = refs[-1]
    moves = [
        pltpu.make_async_copy(src, dst, sem.at[n]) for n, (src, dst) in enumerate(zip(sources, copies))
    ]
    for move in moves:
        move.start()
    for move in moves:
        move.wait()
    w_ref, sty_ref, noise_ref, gain_ref, bias_ref, dw_ref, db_ref, do_ref, rgb_ref = copies
    wslot_ref, stys_ref, demod_ref, nb_ref, disc_ref, rgbp_ref, stycopy_ref = outs
    rgbp_ref[...] = pad_rows(rgb_ref[...], EXTRA)
    stycopy_ref[...] = sty_ref[...]
    chan = idx[1]
    own = w_ref.shape[1]
    full = w_ref.shape[0] // TAPS
    count = sty_ref.shape[0]
    chans = full // own
    for d in range(chans):
        part = chan ^ d
        for k in range(TAPS):
            start = pl.multiple_of(k * full + part * own, own)
            wslot_ref[d * own : (d + 1) * own, k * own : (k + 1) * own] = w_ref[pl.ds(start, own), :]
        stys_ref[:, d * own : (d + 1) * own] = sty_ref[:, pl.ds(pl.multiple_of(part * own, own), own)]
    squares = jnp.zeros((full, own), f32)
    for k in range(TAPS):
        w = w_ref[k * full : (k + 1) * full, :].astype(f32)
        squares = squares + w * w
    sty = sty_ref[...]
    cols = pad_rows(sty * sty, own).T
    for b in range(count):
        total = jnp.sum(cols[:, b : b + 1] * squares, axis=0, keepdims=True)
        demod_ref[b : b + 1, :] = lax.rsqrt(total + epsilon)
        noise = jnp.broadcast_to(noise_ref[b : b + 1, :], (own, PIX)).T
        nb_ref[b * PIX : (b + 1) * PIX, :] = gain_ref[...] * noise + bias_ref[...]
    rows = [dw_ref[0:1, :], dw_ref[1:2, :], dw_ref[2:3, :], db_ref[...], do_ref[...]]
    for n, row in enumerate(rows):
        disc_ref[n] = jnp.broadcast_to(row, (own, row.shape[1])).T


def modulated_products(second, slots, x_refs, stys_ref, wslot_ref, xm_ref):
    count = stys_ref.shape[0]
    own = stys_ref.shape[1] // 4
    for n, d in enumerate(slots):
        for b in range(count):
            sty = stys_ref[b : b + 1, d * own : (d + 1) * own]
            x = x_refs[n][b * PIX : (b + 1) * PIX, :] if second else x_refs[n][b].T
            x = x.astype(f32)
            xm_ref[b * PIX : (b + 1) * PIX, n * own : (n + 1) * own] = (x * sty).astype(bf16)
    w = jnp.concatenate([wslot_ref[d * own : (d + 1) * own, :] for d in slots], axis=0)
    return jnp.dot(xm_ref[...], w, preferred_element_type=f32)


def half_conv_kernel(second, slots, xa_ref, xb_ref, stys_ref, wslot_ref, xm_ref, part_ref):
    part_ref[...] = modulated_products(second, slots, (xa_ref, xb_ref), stys_ref, wslot_ref, xm_ref)


def conv_kernel(second, slots, *refs):
    x_refs = refs[:2]
    stys_ref, wslot_ref, demod_ref, nb_ref, rgb_ref, part_ref = refs[2:8]
    pay_ref, slope_ref, z_ref, xm_ref = refs[8:12]
    count = stys_ref.shape[0]
    own = demod_ref.shape[1]
    pixels = count * PIX
    products = part_ref[...] + modulated_products(second, slots, x_refs, stys_ref, wslot_ref, xm_ref)
    z = None
    for kx in range(3):
        total = None
        for ky in range(3):
            k = 3 * ky + kx
            moved = row_shift(products[:, k * own : (k + 1) * own], ky - 1)
            total = moved if total is None else total + moved
        total = col_shift(total, kx - 1)
        z = total if z is None else z + total
    z_ref[...] = z
    demod = jnp.concatenate(
        [jnp.broadcast_to(demod_ref[b : b + 1, :], (PIX, own)) for b in range(count)], axis=0
    )
    pre = demod * z + nb_ref[...]
    soft, sig = act_parts(pre)
    y = (root_two * (0.2 * pre + 0.8 * soft)).astype(bf16)
    slope_ref[...] = root_two * (0.2 + 0.8 * sig)
    rgb = rgb_ref[...]
    pay_ref[:pixels, :] = y
    pay_ref[pixels:, :] = rgb
    if second:
        refs[12][...] = lax.dot_general(rgb, y, NT, preferred_element_type=f32)[:8]


def image_pair_kernel(own_ref, got_ref, out_ref):
    out_ref[...] = own_ref[...] + got_ref[...]


def first_image_kernel(*refs):
    out_ref = refs[-1]
    pixels = out_ref.shape[1]
    parts = [
        lax.dot_general(ref[pixels:, :], ref[:pixels, :], NT, preferred_element_type=f32)[:8]
        for ref in refs[:4]
    ]
    out_ref[...] = (parts[0] + parts[1]) + (parts[2] + parts[3])


def head_grad(dimage, rgb_ref):
    own = rgb_ref.shape[1]
    hi = dimage.astype(bf16).astype(f32)
    lo = dimage - hi
    left = pad_rows(jnp.concatenate([hi, lo], axis=0), own).T.astype(bf16)
    rgb = rgb_ref[...].astype(f32)[:8]
    right = jnp.concatenate([rgb, rgb], axis=0)
    return jnp.dot(left, pad_rows(right, own).astype(bf16), preferred_element_type=f32)


def store_gz(da, z, demod_ref, pay_ref):
    count, own = demod_ref.shape
    rows = []
    for b in range(count):
        demod = demod_ref[b : b + 1, :]
        part = da[b * PIX : (b + 1) * PIX]
        pay_ref[b * PIX : (b + 1) * PIX, :] = (part * demod).astype(bf16)
        d_demod = jnp.sum(part * z[b * PIX : (b + 1) * PIX], axis=0, keepdims=True)
        rows.append(-d_demod * demod * demod * demod)
    coef = jnp.concatenate(rows + [jnp.zeros((8 - count, own), f32)], axis=0)
    hi = coef.astype(bf16).astype(f32)
    pay_ref[count * PIX :, :] = jnp.concatenate([hi, coef - hi], axis=0).astype(bf16)


def shifted_gz(gz):
    gz = gz.astype(f32)
    by_col = [col_shift(gz, 1 - kx).astype(bf16) for kx in range(3)]
    return jnp.concatenate([row_shift(by_col[k % 3], 1 - k // 3) for k in range(TAPS)], axis=1)


def store_dx(cols, wslot_ref, stys_ref, keep_ref, send_ref):
    count = stys_ref.shape[0]
    own = keep_ref.shape[1]
    share = lax.dot_general(cols, wslot_ref[...], NT, preferred_element_type=f32)
    for d in range(4):
        for b in range(count):
            sty = stys_ref[b : b + 1, d * own : (d + 1) * own]
            block = share[b * PIX : (b + 1) * PIX, d * own : (d + 1) * own] * sty
            at = (d // 2) * count * PIX + b * PIX
            if d % 2 == 0:
                keep_ref[at : at + PIX, :] = block
            else:
                send_ref[at : at + PIX, :] = block.astype(bf16)


def disc_kernel(
    own_ref, other_ref, first_ref, disc_ref, rgb_ref, slope_ref, z_ref, demod_ref,
    wslot_ref, stys_ref, tail_ref, pay_ref, keep_ref, send_ref,
):
    image = (own_ref[...] + other_ref[...]) + first_ref[...]
    lanes = 128
    per = PIX // lanes
    count = stys_ref.shape[0]
    out_rows, logits = [], []
    for b in range(count):
        logit = jnp.zeros((1, 1), f32)
        chunks = []
        for n in range(per):
            at = b * PIX + n * lanes
            q = disc_ref[3]
            for ch in range(3):
                q = q + disc_ref[ch] * image[ch : ch + 1, at : at + lanes]
            soft, sig = act_parts(q)
            hidden = 0.2 * q + 0.8 * soft
            logit = logit + jnp.sum(disc_ref[4] * hidden, keepdims=True)
            dq = (disc_ref[4] / PIX) * (0.2 + 0.8 * sig)
            chunks.append(
                [jnp.sum(disc_ref[ch] * dq, axis=0, keepdims=True) for ch in range(3)]
            )
        logit = logit / PIX
        e = jnp.exp(-jnp.abs(logit))
        under = 1.0 + e
        g = jnp.where(logit >= 0.0, (1.0 - under) / under, e / under - 1.0)
        rows = [jnp.concatenate([c[ch] for c in chunks], axis=1) * g for ch in range(3)]
        out_rows.append(jnp.concatenate(rows + [jnp.zeros((5, PIX), f32)], axis=0))
        wide = jnp.broadcast_to(logit, (1, lanes))
        hi = wide.astype(bf16).astype(f32)
        mid = (wide - hi).astype(bf16).astype(f32)
        logits += [hi, mid, wide - hi - mid]
    dimage = jnp.concatenate(out_rows, axis=1)
    pieces = [
        dimage[ch : ch + 1, n * lanes : (n + 1) * lanes] for ch in range(3) for n in range(count * per)
    ]
    high = jnp.concatenate(pieces, axis=0)
    low = high - high.astype(bf16).astype(f32)
    spare = TAIL - 2 * len(pieces) - len(logits)
    tail_ref[...] = jnp.concatenate(
        [high, low] + logits + [jnp.zeros((spare, lanes), f32)], axis=0
    ).astype(bf16)
    da = head_grad(dimage, rgb_ref) * slope_ref[...]
    store_gz(da, z_ref[...], demod_ref, pay_ref)
    cols = shifted_gz(pay_ref[: count * PIX, :])
    store_dx(cols, wslot_ref, stys_ref, keep_ref, send_ref)


def pair_kernel(keep_ref, got_ref, tail_ref, near_ref, far_ref):
    rows = far_ref.shape[0]
    near_ref[rows:, :] = tail_ref[...]
    near_ref[:rows, :] = (keep_ref[:rows] + got_ref[:rows].astype(f32)).astype(bf16)
    far_ref[...] = (keep_ref[rows:] + got_ref[rows:].astype(f32)).astype(bf16)


def first_grad_kernel(
    idx, s0_ref, s1_ref, rgb_ref, slope_ref, z_ref, demod_ref, other_ref, tail_ref,
    pay_ref, logit_ref,
):
    count = demod_ref.shape[0]
    pixels = count * PIX
    chunks = pixels // 128

    def put_logits(tail):
        for b in range(count):
            at = 6 * chunks + 3 * b
            logit_ref[b] = jnp.max((tail[at : at + 1] + tail[at + 1 : at + 2]) + tail[at + 2 : at + 3])

    @pl.when(idx[0] == 0)
    def _():
        dx = (s0_ref[:pixels, :].astype(f32) + s1_ref[...].astype(f32)).astype(bf16)
        tail = s0_ref[pixels:, :].astype(f32)
        put_logits(tail)
        both = tail[: 3 * chunks] + tail[3 * chunks : 6 * chunks]
        rows = [
            jnp.concatenate(
                [both[ch * chunks + n : ch * chunks + n + 1] for n in range(chunks)], axis=1
            )
            for ch in range(3)
        ]
        dimage = jnp.concatenate(rows + [jnp.zeros((5, pixels), f32)], axis=0)
        da = (head_grad(dimage, rgb_ref) + dx.astype(f32)) * slope_ref[...]
        store_gz(da, z_ref[...], demod_ref, pay_ref)

    @pl.when(idx[0] != 0)
    def _():
        put_logits(tail_ref[...].astype(f32))
        pay_ref[...] = other_ref[...]


def share_kernel(pay_ref, wslot_ref, stys_ref, xm_ref, keep_ref, send_ref, acc_ref):
    cols = shifted_gz(pay_ref[: stys_ref.shape[0] * PIX, :])
    store_dx(cols, wslot_ref, stys_ref, keep_ref, send_ref)
    acc_ref[...] = jnp.dot(xm_ref[: acc_ref.shape[0], :], cols, preferred_element_type=f32)


def dx_pair_kernel(keep_ref, got_ref, near_ref, far_ref):
    rows = near_ref.shape[0]
    near_ref[...] = keep_ref[:rows] + got_ref[:rows].astype(f32)
    far_ref[...] = (keep_ref[rows:] + got_ref[rows:].astype(f32)).astype(bf16)


def turn_kernel(idx, a01_ref, a23_ref, b02_ref, b13_ref, sty_ref, out_ref):
    chan = idx[1]
    full = sty_ref.shape[1]
    count = sty_ref.shape[0]
    own = full // 4

    def turn(ref, slots):
        for n, d in enumerate(slots):
            start = pl.multiple_of((chan ^ d) * own, own)
            out_ref[pl.ds(start, own), :] = ref[:, n * own : (n + 1) * own].T

    @pl.when(idx[0] == 0)
    def _():
        turn(a01_ref, (0, 1))
        turn(a23_ref, (2, 3))

    @pl.when(idx[0] != 0)
    def _():
        turn(b02_ref, (0, 2))
        turn(b13_ref, (1, 3))

    sty = sty_ref[...]
    hi = sty.astype(bf16).astype(f32)
    mid = (sty - hi).astype(bf16).astype(f32)
    lo = sty - hi - mid
    rows = [hi, mid, lo]
    out_ref[full:, :] = jnp.concatenate(
        rows + [jnp.zeros((EXTRA - 3 * count, full), f32)], axis=0
    ).astype(bf16)


def z_partner(z, core):
    return ((z + core) ^ 1) - core


def weight_kernel(
    idx, pay_ref, other_pay_ref, xm_ref, other_xm_ref, w_ref, before_ref,
    keep_ref, send_1_ref, send_2_ref, send_3_ref, sum_ref,
):
    core, y, z = idx[1] & 1, idx[2], idx[3]
    full = before_ref.shape[0]
    own = pay_ref.shape[1]
    pixels = pay_ref.shape[0] - EXTRA
    count = pixels // PIX
    cols = shifted_gz(other_pay_ref[:pixels, :])
    other_xm = other_xm_ref[:full, :]
    sty_rows, coef_rows = [], []
    for pay, xm in ((pay_ref, xm_ref), (other_pay_ref, other_xm_ref)):
        tail = xm[full:, :].astype(f32)
        sty = tail[:count] + tail[count : 2 * count] + tail[2 * count : 3 * count]
        sty_rows.append(sty * sty)
        tail = pay[pixels:, :].astype(f32)
        coef_rows.append(tail[:count] + tail[8 : 8 + count])
    left = pad_rows(jnp.concatenate(sty_rows, axis=0), own).T
    right = pad_rows(jnp.concatenate(coef_rows, axis=0), own)
    demod_term = jnp.dot(left, right, precision=lax.Precision.HIGHEST, preferred_element_type=f32)
    for first in range(0, TAPS, 2):
        taps = range(first, min(first + 2, TAPS))
        lanes = slice(first * own, (taps[-1] + 1) * own)
        total = before_ref[:, lanes] + jnp.dot(
            other_xm, cols[:, lanes], preferred_element_type=f32
        )
        for n, k in enumerate(taps):
            at = slice(k * full, (k + 1) * full)
            w = w_ref[at, :].astype(f32)
            sum_ref[at, :] = total[:, n * own : (n + 1) * own] + w * demod_term
    rows = keep_ref.shape[0] // 4
    step = 1 - 2 * core
    for d, ref in enumerate((keep_ref, send_1_ref, send_2_ref, send_3_ref)):
        to_y = (y + step * d) & 3
        for e in range(4):
            start = (to_y * 8 + ((z + 2 * e) & 7)) * rows
            block = sum_ref[pl.ds(pl.multiple_of(start, RES), rows), :]
            ref[e * rows : (e + 1) * rows, :] = block.astype(ref.dtype)


def y_sum_kernel(keep_ref, r1_ref, r2_ref, r3_ref, own_ref, *out_refs):
    rows = own_ref.shape[0]
    for e, ref in enumerate((own_ref, *out_refs)):
        at = slice(e * rows, (e + 1) * rows)
        total = keep_ref[at] + r1_ref[at].astype(f32)
        total = total + (r2_ref[at].astype(f32) + r3_ref[at].astype(f32))
        ref[...] = total.astype(ref.dtype)


def total_kernel(*refs):
    total = refs[0][...].astype(f32)
    for ref in refs[1:-1]:
        total = total + ref[...].astype(f32)
    refs[-1][...] = total


def input_grad_kernel(near_ref, far_ref, dx_ref):
    dx = (near_ref[...] + far_ref[...].astype(f32)).astype(bf16)
    for b in range(dx_ref.shape[0]):
        dx_ref[b] = dx[b * PIX : (b + 1) * PIX].T


def call(kernel, outs, args, scratch=(), scalars=0, raws=0, keep=True):
    smem = pl.BlockSpec(memory_space=pltpu.SMEM)
    vmem = pl.BlockSpec(memory_space=pltpu.VMEM)
    plain = scalars + raws
    args = (
        list(args[:scalars])
        + [pltpu.with_memory_space_constraint(a, pltpu.HBM) for a in args[scalars:plain]]
        + [pltpu.with_memory_space_constraint(a, pltpu.VMEM) for a in args[plain:]]
    )
    hbm = pl.BlockSpec(memory_space=pltpu.HBM)
    place = pltpu.VMEM if keep else jax.ShapeDtypeStruct
    return pl.pallas_call(
        kernel,
        out_shape=[
            jax.ShapeDtypeStruct(*o[:2]) if len(o) > 2 else place(*o) for o in outs
        ],
        in_specs=[smem] * scalars + [hbm] * raws + [vmem] * (len(args) - plain),
        out_specs=[smem if len(o) > 2 else vmem for o in outs],
        scratch_shapes=list(scratch),
        compiler_params=pltpu.CompilerParams(vmem_limit_bytes=20 * 2**20),
    )(*args)


def body(
    base, style, noise, conv_weight, conv_bias, noise_gain, rgb_weight, disc_weight, disc_bias,
    disc_out,
):
    weight, styles, noises, rgb = conv_weight[0], style[0], noise[0], rgb_weight[0]
    own = weight.shape[1]
    full = weight.shape[0] // TAPS
    count = base.shape[0]
    pixels = count * PIX
    dp_index = lax.axis_index("dp")
    idx = jnp.stack(
        [lax.axis_index("segment"), lax.axis_index("chan"), dp_index // 8, dp_index % 8]
    ).astype(jnp.int32)

    def across(value, links):
        return lax.ppermute(value, ("segment", "chan"), links)

    def by_core(value, place):
        links = []
        for y in range(4):
            for z in range(8):
                for c in range(4):
                    to_y, to_z = place(y, z, c % 2)
                    links.append(((y * 8 + z) * 4 + c, (to_y % 4 * 8 + to_z % 8) * 4 + c))
        return lax.ppermute(value, ("dp", "chan"), links)

    def over_y(value, d):
        return by_core(value, lambda y, z, core: (y - d if core else y + d, z))

    def over_z(value, d):
        return lax.ppermute(
            value, "dp", [(y * 8 + z, y * 8 + (z + d) % 8) for y in range(4) for z in range(8)]
        )

    def flip(value, d):
        return across(value, [(s * 4 + c, (1 - s) * 4 + (c ^ d)) for s in range(2) for c in range(4)])

    def within(value, d):
        return across(value, [(s * 4 + c, s * 4 + (c ^ d)) for s in range(2) for c in range(4)])

    x2 = flip(base, 2)
    x1 = within(base, 1)
    x3 = within(x2, 1)
    sources = [
        weight, styles, noises, noise_gain, conv_bias, disc_weight, disc_bias[None], disc_out[None],
        rgb,
    ]
    wslot, stys, demod, nb, disc, rgbp, sty = call(
        prep_kernel,
        [
            ((full, TAPS * own), bf16),
            ((count, full), f32),
            ((count, own), f32),
            ((pixels, own), f32),
            ((5, disc_weight.shape[1], own), f32),
            ((EXTRA, own), bf16),
            ((count, full), f32),
        ],
        [idx, *sources],
        scratch=[pltpu.VMEM(a.shape, a.dtype) for a in sources]
        + [pltpu.SemaphoreType.DMA((len(sources),))],
        scalars=1,
        raws=len(sources),
    )
    half_outs = [((pixels, full // 2), bf16), ((pixels, TAPS * own), f32)]
    conv_outs = [
        ((pixels + EXTRA, own), bf16),
        ((pixels, own), f32),
        ((pixels, own), f32),
        half_outs[0],
    ]
    xm_a01, part_a = call(
        functools.partial(half_conv_kernel, False, (0, 1)), half_outs, [base, x1, stys, wslot]
    )
    pay, slope_a, z_a, xm_a23 = call(
        functools.partial(conv_kernel, False, (2, 3)),
        conv_outs,
        [x2, x3, stys, wslot, demod, nb, rgbp, part_a],
    )
    y0 = flip(pay, 0)
    y2 = flip(pay, 2)
    y1 = within(y0, 1)
    y3 = within(y2, 1)
    xm_b02, part_b = call(
        functools.partial(half_conv_kernel, True, (0, 2)), half_outs, [y0, y2, stys, wslot]
    )
    _, slope_b, z_b, xm_b13, image_own = call(
        functools.partial(conv_kernel, True, (1, 3)),
        conv_outs + [((8, pixels), f32)],
        [y1, y3, stys, wslot, demod, nb, rgbp, part_b],
    )
    image_got = within(image_own, 1)
    (image_chip,) = call(image_pair_kernel, [((8, pixels), f32)], [image_own, image_got])
    image_other = within(image_chip, 2)
    (xm,) = call(
        turn_kernel,
        [((full + EXTRA, pixels), bf16)],
        [idx, xm_a01, xm_a23, xm_b02, xm_b13, sty],
        scalars=1,
    )
    (image_first,) = call(first_image_kernel, [((8, pixels), f32)], [y0, y1, y2, y3])

    def to_partner(value):
        return by_core(value, lambda y, z, core: (y, z_partner(z, core)))

    other_xm = to_partner(xm)
    two = (2 * pixels, own)
    tail, pay_b, dx_keep, dx_send = call(
        disc_kernel,
        [((TAIL, own), bf16), ((pixels + EXTRA, own), bf16), (two, f32), (two, bf16)],
        [image_chip, image_other, image_first, disc, rgbp, slope_b, z_b, demod, wslot, stys],
    )
    dx_got = within(dx_send, 1)
    share = ((pixels, own), bf16)
    dx_near, dx_far = call(
        pair_kernel, [((pixels + TAIL, own), bf16), share], [dx_keep, dx_got, tail]
    )
    got = [flip(dx_near, 0), flip(dx_far, 2)]
    pay_g, logits = call(
        first_grad_kernel,
        [((pixels + EXTRA, own), bf16), ((count,), f32, True)],
        [idx, *got, rgbp, slope_a, z_a, demod, pay_b, tail],
        scalars=1,
    )
    other_pay = to_partner(pay_g)
    keep, send, before = call(
        share_kernel, [(two, f32), (two, bf16), ((full, TAPS * own), f32)], [pay_g, wslot, stys, xm]
    )
    got = within(send, 1)
    near, far = call(dx_pair_kernel, [((pixels, own), f32), share], [keep, got])
    mine = [near, within(far, 2)]
    rows = weight.shape[0] // 32
    four = (4 * rows, own)
    y_keep, *y_send = call(
        weight_kernel,
        [(four, f32)] + [(four, bf16)] * 3,
        [idx, pay_g, other_pay, xm, other_xm, weight, before],
        scratch=[pltpu.VMEM(weight.shape, f32)],
        scalars=1,
    )
    y_got = [over_y(y_send[d - 1], d) for d in (1, 2, 3)]
    block = (rows, own)
    z_own, *z_outs = call(y_sum_kernel, [(block, f32)] + [(block, bf16)] * 3, [y_keep, *y_got])
    parts = [z_own] + [over_z(z_outs[e - 1], 2 * e) for e in (1, 2, 3)]
    (dx,) = call(input_grad_kernel, [((count, own, PIX), bf16)], mine, keep=False)
    (grad_rows,) = call(total_kernel, [((rows, own), f32)], parts, keep=False)
    return (grad_rows[None], logits, dx[None])


def solution(mesh):
    placed = (
        P("dp", "chan", None),
        P("segment", "dp", None),
        P("segment", "dp", None),
        P("segment", None, "chan"),
        P("segment", "chan"),
        P("segment", "chan"),
        P("segment", None, "chan"),
        P(),
        P(),
        P(),
    )
    return jax.shard_map(
        body,
        mesh=mesh,
        in_specs=placed,
        out_specs=(P("segment", "dp", "chan"), P("dp"), P("segment", "dp", "chan", None)),
        check_vma=False,
    )
```

```python
import functools

import jax
import jax.numpy as jnp
from jax import lax
from jax.experimental import pallas as pl
from jax.experimental.pallas import tpu as pltpu
from jax.sharding import PartitionSpec as P


RES = 16
PIX = RES * RES
TAPS = 9
EXTRA = 16
TAIL = 32
epsilon = 1e-06
root_two = 1.4142135623730951
f32 = jnp.float32
bf16 = jnp.bfloat16


NT = (((1,), (1,)), ((), ()))


def act_parts(t):
    e = jnp.exp(-jnp.abs(t))
    r = 1.0 / (1.0 + e)
    soft = jnp.maximum(t, 0.0) + jnp.log(1.0 + e)
    sig = jnp.where(t >= 0.0, r, e * r)
    return soft, sig


def row_shift(v, a):
    if a == 0:
        return v
    zeros = jnp.zeros((RES, v.shape[1]), v.dtype)
    parts = []
    for b in range(v.shape[0] // PIX):
        base = b * PIX
        if a > 0:
            parts += [v[base + RES : base + PIX], zeros]
        else:
            parts += [zeros, v[base : base + PIX - RES]]
    return jnp.concatenate(parts, axis=0)


def col_shift(v, b):
    if b == 0:
        return v
    x = lax.broadcasted_iota(jnp.int32, v.shape, 0) & (RES - 1)
    if b > 0:
        return jnp.where(x < RES - 1, pltpu.roll(v, v.shape[0] - 1, 0), 0.0)
    return jnp.where(x > 0, pltpu.roll(v, 1, 0), 0.0)


def pad_rows(v, rows):
    return jnp.concatenate([v, jnp.zeros((rows - v.shape[0], v.shape[1]), v.dtype)], axis=0)


def prep_kernel(idx, *refs):
    number = (len(refs) - 8) // 2
    sources, outs, copies = refs[:number], refs[number : number + 7], refs[number + 7 : -1]
    sem = refs[-1]
    moves = [
        pltpu.make_async_copy(src, dst, sem.at[n]) for n, (src, dst) in enumerate(zip(sources, copies))
    ]
    for move in moves:
        move.start()
    for move in moves:
        move.wait()
    w_ref, sty_ref, noise_ref, gain_ref, bias_ref, dw_ref, db_ref, do_ref, rgb_ref = copies
    wslot_ref, stys_ref, demod_ref, nb_ref, disc_ref, rgbp_ref, stycopy_ref = outs
    rgbp_ref[...] = pad_rows(rgb_ref[...], EXTRA)
    stycopy_ref[...] = sty_ref[...]
    chan = idx[1]
    own = w_ref.shape[1]
    full = w_ref.shape[0] // TAPS
    count = sty_ref.shape[0]
    chans = full // own
    for d in range(chans):
        part = chan ^ d
        for k in range(TAPS):
            start = pl.multiple_of(k * full + part * own, own)
            wslot_ref[d * own : (d + 1) * own, k * own : (k + 1) * own] = w_ref[pl.ds(start, own), :]
        stys_ref[:, d * own : (d + 1) * own] = sty_ref[:, pl.ds(pl.multiple_of(part * own, own), own)]
    squares = jnp.zeros((full, own), f32)
    for k in range(TAPS):
        w = w_ref[k * full : (k + 1) * full, :].astype(f32)
        squares = squares + w * w
    sty = sty_ref[...]
    cols = pad_rows(sty * sty, own).T
    for b in range(count):
        total = jnp.sum(cols[:, b : b + 1] * squares, axis=0, keepdims=True)
        demod_ref[b : b + 1, :] = lax.rsqrt(total + epsilon)
        noise = jnp.broadcast_to(noise_ref[b : b + 1, :], (own, PIX)).T
        nb_ref[b * PIX : (b + 1) * PIX, :] = gain_ref[...] * noise + bias_ref[...]
    rows = [dw_ref[0:1, :], dw_ref[1:2, :], dw_ref[2:3, :], db_ref[...], do_ref[...]]
    for n, row in enumerate(rows):
        disc_ref[n] = jnp.broadcast_to(row, (own, row.shape[1])).T


def modulated_products(second, slots, x_refs, stys_ref, wslot_ref, xm_ref):
    count = stys_ref.shape[0]
    own = stys_ref.shape[1] // 4
    for n, d in enumerate(slots):
        for b in range(count):
            sty = stys_ref[b : b + 1, d * own : (d + 1) * own]
            x = x_refs[n][b * PIX : (b + 1) * PIX, :] if second else x_refs[n][b].T
            x = x.astype(f32)
            xm_ref[b * PIX : (b + 1) * PIX, n * own : (n + 1) * own] = (x * sty).astype(bf16)
    w = jnp.concatenate([wslot_ref[d * own : (d + 1) * own, :] for d in slots], axis=0)
    return jnp.dot(xm_ref[...], w, preferred_element_type=f32)


def half_conv_kernel(second, slots, xa_ref, xb_ref, stys_ref, wslot_ref, xm_ref, part_ref):
    part_ref[...] = modulated_products(second, slots, (xa_ref, xb_ref), stys_ref, wslot_ref, xm_ref)


def conv_kernel(second, slots, *refs):
    x_refs = refs[:2]
    stys_ref, wslot_ref, demod_ref, nb_ref, rgb_ref, part_ref = refs[2:8]
    pay_ref, slope_ref, z_ref, xm_ref = refs[8:12]
    count = stys_ref.shape[0]
    own = demod_ref.shape[1]
    pixels = count * PIX
    products = part_ref[...] + modulated_products(second, slots, x_refs, stys_ref, wslot_ref, xm_ref)
    z = None
    for kx in range(3):
        total = None
        for ky in range(3):
            k = 3 * ky + kx
            moved = row_shift(products[:, k * own : (k + 1) * own], ky - 1)
            total = moved if total is None else total + moved
        total = col_shift(total, kx - 1)
        z = total if z is None else z + total
    z_ref[...] = z
    demod = jnp.concatenate(
        [jnp.broadcast_to(demod_ref[b : b + 1, :], (PIX, own)) for b in range(count)], axis=0
    )
    pre = demod * z + nb_ref[...]
    soft, sig = act_parts(pre)
    y = (root_two * (0.2 * pre + 0.8 * soft)).astype(bf16)
    slope_ref[...] = root_two * (0.2 + 0.8 * sig)
    rgb = rgb_ref[...]
    pay_ref[:pixels, :] = y
    pay_ref[pixels:, :] = rgb


def own_image_kernel(pay_ref, out_ref):
    pixels = out_ref.shape[1]
    out_ref[...] = lax.dot_general(
        pay_ref[pixels:, :], pay_ref[:pixels, :], NT, preferred_element_type=f32
    )[:8]


def image_pair_kernel(own_ref, got_ref, out_ref):
    out_ref[...] = own_ref[...] + got_ref[...]


def first_image_kernel(*refs):
    out_ref = refs[-1]
    pixels = out_ref.shape[1]
    parts = [
        lax.dot_general(ref[pixels:, :], ref[:pixels, :], NT, preferred_element_type=f32)[:8]
        for ref in refs[:4]
    ]
    out_ref[...] = (parts[0] + parts[1]) + (parts[2] + parts[3])


def head_grad(dimage, rgb_ref):
    own = rgb_ref.shape[1]
    hi = dimage.astype(bf16).astype(f32)
    lo = dimage - hi
    left = pad_rows(jnp.concatenate([hi, lo], axis=0), own).T.astype(bf16)
    rgb = rgb_ref[...].astype(f32)[:8]
    right = jnp.concatenate([rgb, rgb], axis=0)
    return jnp.dot(left, pad_rows(right, own).astype(bf16), preferred_element_type=f32)


def store_gz(da, z, demod_ref, pay_ref):
    count, own = demod_ref.shape
    rows = []
    for b in range(count):
        demod = demod_ref[b : b + 1, :]
        part = da[b * PIX : (b + 1) * PIX]
        pay_ref[b * PIX : (b + 1) * PIX, :] = (part * demod).astype(bf16)
        d_demod = jnp.sum(part * z[b * PIX : (b + 1) * PIX], axis=0, keepdims=True)
        rows.append(-d_demod * demod * demod * demod)
    coef = jnp.concatenate(rows + [jnp.zeros((8 - count, own), f32)], axis=0)
    hi = coef.astype(bf16).astype(f32)
    pay_ref[count * PIX :, :] = jnp.concatenate([hi, coef - hi], axis=0).astype(bf16)


def shifted_gz(gz):
    gz = gz.astype(f32)
    by_col = [col_shift(gz, 1 - kx).astype(bf16) for kx in range(3)]
    return jnp.concatenate([row_shift(by_col[k % 3], 1 - k // 3) for k in range(TAPS)], axis=1)


def store_dx(cols, wslot_ref, stys_ref, keep_ref, send_ref):
    count = stys_ref.shape[0]
    own = keep_ref.shape[1]
    share = lax.dot_general(cols, wslot_ref[...], NT, preferred_element_type=f32)
    for d in range(4):
        for b in range(count):
            sty = stys_ref[b : b + 1, d * own : (d + 1) * own]
            block = share[b * PIX : (b + 1) * PIX, d * own : (d + 1) * own] * sty
            at = (d // 2) * count * PIX + b * PIX
            if d % 2 == 0:
                keep_ref[at : at + PIX, :] = block
            else:
                send_ref[at : at + PIX, :] = block.astype(bf16)


def disc_kernel(
    own_ref, other_ref, first_ref, disc_ref, rgb_ref, slope_ref, z_ref, demod_ref,
    wslot_ref, stys_ref, tail_ref, pay_ref, keep_ref, send_ref,
):
    image = (own_ref[...] + other_ref[...]) + first_ref[...]
    lanes = 128
    per = PIX // lanes
    count = stys_ref.shape[0]
    out_rows, logits = [], []
    for b in range(count):
        logit = jnp.zeros((1, 1), f32)
        chunks = []
        for n in range(per):
            at = b * PIX + n * lanes
            q = disc_ref[3]
            for ch in range(3):
                q = q + disc_ref[ch] * image[ch : ch + 1, at : at + lanes]
            soft, sig = act_parts(q)
            hidden = 0.2 * q + 0.8 * soft
            logit = logit + jnp.sum(disc_ref[4] * hidden, keepdims=True)
            dq = (disc_ref[4] / PIX) * (0.2 + 0.8 * sig)
            chunks.append(
                [jnp.sum(disc_ref[ch] * dq, axis=0, keepdims=True) for ch in range(3)]
            )
        logit = logit / PIX
        e = jnp.exp(-jnp.abs(logit))
        under = 1.0 + e
        g = jnp.where(logit >= 0.0, 1.0 / under, e / under) - 1.0
        rows = [jnp.concatenate([c[ch] for c in chunks], axis=1) * g for ch in range(3)]
        out_rows.append(jnp.concatenate(rows + [jnp.zeros((5, PIX), f32)], axis=0))
        wide = jnp.broadcast_to(logit, (1, lanes))
        hi = wide.astype(bf16).astype(f32)
        mid = (wide - hi).astype(bf16).astype(f32)
        logits += [hi, mid, wide - hi - mid]
    dimage = jnp.concatenate(out_rows, axis=1)
    pieces = [
        dimage[ch : ch + 1, n * lanes : (n + 1) * lanes] for ch in range(3) for n in range(count * per)
    ]
    high = jnp.concatenate(pieces, axis=0)
    low = high - high.astype(bf16).astype(f32)
    spare = TAIL - 2 * len(pieces) - len(logits)
    tail_ref[...] = jnp.concatenate(
        [high, low] + logits + [jnp.zeros((spare, lanes), f32)], axis=0
    ).astype(bf16)
    da = head_grad(dimage, rgb_ref) * slope_ref[...]
    store_gz(da, z_ref[...], demod_ref, pay_ref)
    cols = shifted_gz(pay_ref[: count * PIX, :])
    store_dx(cols, wslot_ref, stys_ref, keep_ref, send_ref)


def pair_kernel(keep_ref, got_ref, tail_ref, near_ref, far_ref):
    rows = far_ref.shape[0]
    near_ref[rows:, :] = tail_ref[...]
    near_ref[:rows, :] = (keep_ref[:rows] + got_ref[:rows].astype(f32)).astype(bf16)
    far_ref[...] = (keep_ref[rows:] + got_ref[rows:].astype(f32)).astype(bf16)


def first_grad_kernel(
    idx, s0_ref, s1_ref, rgb_ref, slope_ref, z_ref, demod_ref, other_ref, pay_ref,
):
    count = demod_ref.shape[0]
    pixels = count * PIX
    chunks = pixels // 128

    @pl.when(idx[0] == 0)
    def _():
        dx = (s0_ref[:pixels, :].astype(f32) + s1_ref[...].astype(f32)).astype(bf16)
        tail = s0_ref[pixels:, :].astype(f32)
        both = tail[: 3 * chunks] + tail[3 * chunks : 6 * chunks]
        rows = [
            jnp.concatenate(
                [both[ch * chunks + n : ch * chunks + n + 1] for n in range(chunks)], axis=1
            )
            for ch in range(3)
        ]
        dimage = jnp.concatenate(rows + [jnp.zeros((5, pixels), f32)], axis=0)
        da = (head_grad(dimage, rgb_ref) + dx.astype(f32)) * slope_ref[...]
        store_gz(da, z_ref[...], demod_ref, pay_ref)

    @pl.when(idx[0] != 0)
    def _():
        pay_ref[...] = other_ref[...]


def share_kernel(pay_ref, wslot_ref, stys_ref, xm_ref, keep_ref, send_ref, acc_ref):
    cols = shifted_gz(pay_ref[: stys_ref.shape[0] * PIX, :])
    store_dx(cols, wslot_ref, stys_ref, keep_ref, send_ref)
    acc_ref[...] = jnp.dot(xm_ref[: acc_ref.shape[0], :], cols, preferred_element_type=f32)


def logits_kernel(idx, s0_ref, tail_ref, logit_ref):
    count = logit_ref.shape[0]
    pixels = count * PIX
    chunks = pixels // 128

    def put(tail):
        for b in range(count):
            at = 6 * chunks + 3 * b
            logit_ref[b] = jnp.max((tail[at : at + 1] + tail[at + 1 : at + 2]) + tail[at + 2 : at + 3])

    @pl.when(idx[0] == 0)
    def _():
        put(s0_ref[pixels:, :].astype(f32))

    @pl.when(idx[0] != 0)
    def _():
        put(tail_ref[...].astype(f32))


def dx_pair_kernel(keep_ref, got_ref, near_ref, far_ref):
    rows = near_ref.shape[0]
    near_ref[...] = keep_ref[:rows] + got_ref[:rows].astype(f32)
    far_ref[...] = (keep_ref[rows:] + got_ref[rows:].astype(f32)).astype(bf16)


def turn_kernel(idx, a01_ref, a23_ref, b02_ref, b13_ref, sty_ref, out_ref):
    chan = idx[1]
    full = sty_ref.shape[1]
    count = sty_ref.shape[0]
    own = full // 4

    def turn(ref, slots):
        for n, d in enumerate(slots):
            start = pl.multiple_of((chan ^ d) * own, own)
            out_ref[pl.ds(start, own), :] = ref[:, n * own : (n + 1) * own].T

    @pl.when(idx[0] == 0)
    def _():
        turn(a01_ref, (0, 1))
        turn(a23_ref, (2, 3))

    @pl.when(idx[0] != 0)
    def _():
        turn(b02_ref, (0, 2))
        turn(b13_ref, (1, 3))

    sty = sty_ref[...]
    hi = sty.astype(bf16).astype(f32)
    mid = (sty - hi).astype(bf16).astype(f32)
    lo = sty - hi - mid
    rows = [hi, mid, lo]
    out_ref[full:, :] = jnp.concatenate(
        rows + [jnp.zeros((EXTRA - 3 * count, full), f32)], axis=0
    ).astype(bf16)


def z_partner(z, core):
    return ((z + core) ^ 1) - core


def weight_kernel(
    idx, pay_ref, other_pay_ref, xm_ref, other_xm_ref, w_ref, before_ref,
    keep_ref, send_1_ref, send_2_ref, send_3_ref, sum_ref,
):
    core, y, z = idx[1] & 1, idx[2], idx[3]
    full = before_ref.shape[0]
    own = pay_ref.shape[1]
    pixels = pay_ref.shape[0] - EXTRA
    count = pixels // PIX
    cols = shifted_gz(other_pay_ref[:pixels, :])
    other_xm = other_xm_ref[:full, :]
    sty_rows, coef_rows = [], []
    for pay, xm in ((pay_ref, xm_ref), (other_pay_ref, other_xm_ref)):
        tail = xm[full:, :].astype(f32)
        sty = tail[:count] + tail[count : 2 * count] + tail[2 * count : 3 * count]
        sty_rows.append(sty * sty)
        tail = pay[pixels:, :].astype(f32)
        coef_rows.append(tail[:count] + tail[8 : 8 + count])
    sty = jnp.concatenate(sty_rows, axis=0)
    coef = jnp.concatenate(coef_rows, axis=0)
    sty_high = sty.astype(bf16).astype(f32)
    coef_high = coef.astype(bf16).astype(f32)
    left = jnp.concatenate([sty_high, sty_high, sty - sty_high, sty - sty_high], axis=0)
    right = jnp.concatenate([coef_high, coef - coef_high, coef_high, coef - coef_high], axis=0)
    demod_term = jnp.dot(
        pad_rows(left, own).T.astype(bf16),
        pad_rows(right, own).astype(bf16),
        preferred_element_type=f32,
    )
    for first in range(0, TAPS, 2):
        taps = range(first, min(first + 2, TAPS))
        lanes = slice(first * own, (taps[-1] + 1) * own)
        total = before_ref[:, lanes] + jnp.dot(
            other_xm, cols[:, lanes], preferred_element_type=f32
        )
        for n, k in enumerate(taps):
            at = slice(k * full, (k + 1) * full)
            w = w_ref[at, :].astype(f32)
            sum_ref[at, :] = (total[:, n * own : (n + 1) * own] + w * demod_term).astype(bf16)
    rows = keep_ref.shape[0] // 4
    step = 1 - 2 * core
    for d, ref in enumerate((keep_ref, send_1_ref, send_2_ref, send_3_ref)):
        to_y = (y + step * d) & 3
        for e in range(4):
            start = (to_y * 8 + ((z + 2 * e) & 7)) * rows
            block = sum_ref[pl.ds(pl.multiple_of(start, RES), rows), :]
            ref[e * rows : (e + 1) * rows, :] = block


def y_sum_kernel(keep_ref, r1_ref, r2_ref, r3_ref, own_ref, *out_refs):
    rows = own_ref.shape[0]
    for e, ref in enumerate((own_ref, *out_refs)):
        at = slice(e * rows, (e + 1) * rows)
        total = keep_ref[at].astype(f32) + r1_ref[at].astype(f32)
        total = total + (r2_ref[at].astype(f32) + r3_ref[at].astype(f32))
        ref[...] = total.astype(ref.dtype)


def total_kernel(*refs):
    total = refs[0][...].astype(f32)
    for ref in refs[1:-1]:
        total = total + ref[...].astype(f32)
    refs[-1][...] = total


def input_grad_kernel(near_ref, far_ref, dx_ref):
    dx = (near_ref[...] + far_ref[...].astype(f32)).astype(bf16)
    for b in range(dx_ref.shape[0]):
        dx_ref[b] = dx[b * PIX : (b + 1) * PIX].T


def call(kernel, outs, args, scratch=(), scalars=0, raws=0, keep=True):
    smem = pl.BlockSpec(memory_space=pltpu.SMEM)
    vmem = pl.BlockSpec(memory_space=pltpu.VMEM)
    plain = scalars + raws
    args = (
        list(args[:scalars])
        + [pltpu.with_memory_space_constraint(a, pltpu.HBM) for a in args[scalars:plain]]
        + [pltpu.with_memory_space_constraint(a, pltpu.VMEM) for a in args[plain:]]
    )
    hbm = pl.BlockSpec(memory_space=pltpu.HBM)
    place = pltpu.VMEM if keep else jax.ShapeDtypeStruct
    return pl.pallas_call(
        kernel,
        out_shape=[
            jax.ShapeDtypeStruct(*o[:2]) if len(o) > 2 else place(*o) for o in outs
        ],
        in_specs=[smem] * scalars + [hbm] * raws + [vmem] * (len(args) - plain),
        out_specs=[smem if len(o) > 2 else vmem for o in outs],
        scratch_shapes=list(scratch),
        compiler_params=pltpu.CompilerParams(vmem_limit_bytes=20 * 2**20),
    )(*args)


def body(
    base, style, noise, conv_weight, conv_bias, noise_gain, rgb_weight, disc_weight, disc_bias,
    disc_out,
):
    weight, styles, noises, rgb = conv_weight[0], style[0], noise[0], rgb_weight[0]
    own = weight.shape[1]
    full = weight.shape[0] // TAPS
    count = base.shape[0]
    pixels = count * PIX
    dp_index = lax.axis_index("dp")
    idx = jnp.stack(
        [lax.axis_index("segment"), lax.axis_index("chan"), dp_index // 8, dp_index % 8]
    ).astype(jnp.int32)

    def across(value, links):
        return lax.ppermute(value, ("segment", "chan"), links)

    def by_core(value, place):
        links = []
        for y in range(4):
            for z in range(8):
                for c in range(4):
                    to_y, to_z = place(y, z, c % 2)
                    links.append(((y * 8 + z) * 4 + c, (to_y % 4 * 8 + to_z % 8) * 4 + c))
        return lax.ppermute(value, ("dp", "chan"), links)

    def over_y(value, d):
        return by_core(value, lambda y, z, core: (y - d if core else y + d, z))

    def over_z(value, d):
        return lax.ppermute(
            value, "dp", [(y * 8 + z, y * 8 + (z + d) % 8) for y in range(4) for z in range(8)]
        )

    def flip(value, d):
        return across(value, [(s * 4 + c, (1 - s) * 4 + (c ^ d)) for s in range(2) for c in range(4)])

    def within(value, d):
        return across(value, [(s * 4 + c, s * 4 + (c ^ d)) for s in range(2) for c in range(4)])

    x2 = flip(base, 2)
    x1 = within(base, 1)
    x3 = within(x2, 1)
    sources = [
        weight, styles, noises, noise_gain, conv_bias, disc_weight, disc_bias[None], disc_out[None],
        rgb,
    ]
    wslot, stys, demod, nb, disc, rgbp, sty = call(
        prep_kernel,
        [
            ((full, TAPS * own), bf16),
            ((count, full), f32),
            ((count, own), f32),
            ((pixels, own), f32),
            ((5, disc_weight.shape[1], own), f32),
            ((EXTRA, own), bf16),
            ((count, full), f32),
        ],
        [idx, *sources],
        scratch=[pltpu.VMEM(a.shape, a.dtype) for a in sources]
        + [pltpu.SemaphoreType.DMA((len(sources),))],
        scalars=1,
        raws=len(sources),
    )
    half_outs = [((pixels, full // 2), bf16), ((pixels, TAPS * own), f32)]
    conv_outs = [
        ((pixels + EXTRA, own), bf16),
        ((pixels, own), f32),
        ((pixels, own), f32),
        half_outs[0],
    ]
    xm_a01, part_a = call(
        functools.partial(half_conv_kernel, False, (0, 1)), half_outs, [base, x1, stys, wslot]
    )
    pay, slope_a, z_a, xm_a23 = call(
        functools.partial(conv_kernel, False, (2, 3)),
        conv_outs,
        [x2, x3, stys, wslot, demod, nb, rgbp, part_a],
    )
    y0 = flip(pay, 0)
    y2 = flip(pay, 2)
    y1 = within(y0, 1)
    y3 = within(y2, 1)
    xm_b02, part_b = call(
        functools.partial(half_conv_kernel, True, (0, 2)), half_outs, [y0, y2, stys, wslot]
    )
    pay_last, slope_b, z_b, xm_b13 = call(
        functools.partial(conv_kernel, True, (1, 3)),
        conv_outs,
        [y1, y3, stys, wslot, demod, nb, rgbp, part_b],
    )
    (image_own,) = call(own_image_kernel, [((8, pixels), f32)], [pay_last])
    image_got = within(image_own, 1)
    (image_chip,) = call(image_pair_kernel, [((8, pixels), f32)], [image_own, image_got])
    image_other = within(image_chip, 2)
    (xm,) = call(
        turn_kernel,
        [((full + EXTRA, pixels), bf16)],
        [idx, xm_a01, xm_a23, xm_b02, xm_b13, sty],
        scalars=1,
    )
    (image_first,) = call(first_image_kernel, [((8, pixels), f32)], [y0, y1, y2, y3])

    def to_partner(value):
        return by_core(value, lambda y, z, core: (y, z_partner(z, core)))

    other_xm = to_partner(xm)
    two = (2 * pixels, own)
    tail, pay_b, dx_keep, dx_send = call(
        disc_kernel,
        [((TAIL, own), bf16), ((pixels + EXTRA, own), bf16), (two, f32), (two, bf16)],
        [image_chip, image_other, image_first, disc, rgbp, slope_b, z_b, demod, wslot, stys],
    )
    dx_got = within(dx_send, 1)
    share = ((pixels, own), bf16)
    dx_near, dx_far = call(
        pair_kernel, [((pixels + TAIL, own), bf16), share], [dx_keep, dx_got, tail]
    )
    got = [flip(dx_near, 0), flip(dx_far, 2)]
    (pay_g,) = call(
        first_grad_kernel,
        [((pixels + EXTRA, own), bf16)],
        [idx, *got, rgbp, slope_a, z_a, demod, pay_b],
        scalars=1,
    )
    (logits,) = call(logits_kernel, [((count,), f32, True)], [idx, got[0], tail], scalars=1)
    other_pay = to_partner(pay_g)
    keep, send, before = call(
        share_kernel, [(two, f32), (two, bf16), ((full, TAPS * own), f32)], [pay_g, wslot, stys, xm]
    )
    got = within(send, 1)
    near, far = call(dx_pair_kernel, [((pixels, own), f32), share], [keep, got])
    mine = [near, within(far, 2)]
    rows = weight.shape[0] // 32
    four = (4 * rows, own)
    y_keep, *y_send = call(
        weight_kernel,
        [(four, bf16)] * 4,
        [idx, pay_g, other_pay, xm, other_xm, weight, before],
        scratch=[pltpu.VMEM(weight.shape, bf16)],
        scalars=1,
    )
    y_got = [over_y(y_send[d - 1], d) for d in (1, 2, 3)]
    block = (rows, own)
    z_own, *z_outs = call(y_sum_kernel, [(block, f32)] + [(block, bf16)] * 3, [y_keep, *y_got])
    parts = [z_own] + [over_z(z_outs[e - 1], 2 * e) for e in (1, 2, 3)]
    (dx,) = call(input_grad_kernel, [((count, own, PIX), bf16)], mine, keep=False)
    (grad_rows,) = call(total_kernel, [((rows, own), f32)], parts, keep=False)
    return (grad_rows[None], logits, dx[None])


def solution(mesh):
    placed = (
        P("dp", "chan", None),
        P("segment", "dp", None),
        P("segment", "dp", None),
        P("segment", None, "chan"),
        P("segment", "chan"),
        P("segment", "chan"),
        P("segment", None, "chan"),
        P(),
        P(),
        P(),
    )
    return jax.shard_map(
        body,
        mesh=mesh,
        in_specs=placed,
        out_specs=(P("segment", "dp", "chan"), P("dp"), P("segment", "dp", "chan", None)),
        check_vma=False,
    )
```
